32 devices in a mesh: segment: 4 (over x, core), lat: 8 (over z, y).
Axes of the slice: x: 2, y: 2, z: 4, core: 2. Of those that a mesh axis runs over, the one named last changes fastest.
Arguments:
- pixels: bfloat16 [4, 4, 5, 64, 128], P(None, None, None, 'lat'), may hold values from -6 to 6
- embed_weight: bfloat16 [80, 512], replicated, may hold values from -0.625 to 0.625
- level_code: bfloat16 [4, 512], replicated, may hold values from -6 to 6
- depth_kernel: bfloat16 [4, 2, 25, 512], P('segment'), may hold values from -1.25 to 1.25
- norm_gain: bfloat16 [4, 2, 512], P('segment'), may hold values from 0.099609375 to 1.8984375
- up_weight: bfloat16 [4, 2, 512, 1024], P('segment'), may hold values from -0.25 to 0.25
- up_bias: bfloat16 [4, 2, 1024], P('segment'), may hold values from -3 to 3
- down_weight: bfloat16 [4, 2, 1024, 512], P('segment'), may hold values from -0.1875 to 0.1875
- down_bias: bfloat16 [4, 2, 512], P('segment'), may hold values from -3 to 3
- fold_gain: bfloat16 [512], replicated, may hold values from 0.099609375 to 1.8984375
- latents: bfloat16 [3, 512], replicated, may hold values from -6 to 6
- memory_weight: bfloat16 [512, 1024], replicated, may hold values from -0.25 to 0.25
- output_weight: bfloat16 [512, 512], replicated, may hold values from -0.25 to 0.25
Outputs:
- latents_out: bfloat16 [4, 16, 32, 3, 512], P('segment', 'lat')
The draws below stay inside these ranges and needn't reach their ends.
All inputs are finite; a program needn't handle non-finite values.
Results may differ from the reference program's by a relative error of at most 0.014.
Values may be sent and summed in bfloat16 or wider, within the bound.
No kernel may reach another device: no remote copies, remote signals or barrier semaphores. Data moves between devices by JAX's collectives and lax.ppermute only.
A program may use at most 64 MiB of HBM per device.

```python
import jax
import jax.numpy as jnp
from jax import lax

D = 512
HID = 1024
HEADS = 16
HSZ = 32
VARS = 5
PATCH = 4
LV = 4
NLAT = 3
BLOCKS = 2
COLS = 32
SECTIONS = 4
MICRO = 4
NR = 16


def level_of(own_key, dims, split, low, largest):
    level = 1.0
    for dim, blocks in split:
        heights = jax.random.uniform(jax.random.fold_in(jax.random.fold_in(own_key, 6), dim), (blocks,), jnp.float32, low / len(split), largest / len(split))
        level = level * jnp.repeat(jnp.exp(heights), dims[dim] // blocks).reshape((-1,) + (1,) * (len(dims) - 1 - dim))
    return level


def scatter_about(key, dims, spread, bound, cuts=(), dtype=jnp.bfloat16):
    entries = spread * jax.random.normal(key, dims, jnp.float32)
    if cuts:
        entries = entries * level_of(key, dims, cuts, -0.22, 0.18)
    return jnp.clip(entries, -bound, bound).astype(dtype)


def setup_inputs(seed: int = 0) -> dict:
    splits = jax.random.split(jax.random.key(seed), 14)
    pixels = scatter_about(splits[0], (MICRO, LV, VARS, NR * PATCH, COLS * PATCH), 1.0, 6.0, ((3, 8),))
    embed_weight = scatter_about(splits[1], (VARS * PATCH * PATCH, D), (VARS * PATCH * PATCH) ** -0.5, 0.625)
    level_code = scatter_about(splits[2], (LV, D), 1.0, 6.0)
    depth_kernel = scatter_about(splits[3], (SECTIONS, BLOCKS, 25, D), 25 ** -0.5, 1.25, ((0, 4),))
    norm_gain = jnp.clip(1.0 + 0.18 * jax.random.normal(splits[4], (SECTIONS, BLOCKS, D), jnp.float32), 0.099609375, 1.8984375).astype(jnp.bfloat16)
    up_weight = scatter_about(splits[5], (SECTIONS, BLOCKS, D, HID), D ** -0.5, 0.25, ((0, 4),))
    up_bias = scatter_about(splits[6], (SECTIONS, BLOCKS, HID), 0.5, 3.0, ((0, 4),))
    down_weight = scatter_about(splits[7], (SECTIONS, BLOCKS, HID, D), HID ** -0.5, 0.1875, ((0, 4),))
    down_bias = scatter_about(splits[8], (SECTIONS, BLOCKS, D), 0.5, 3.0, ((0, 4),))
    fold_gain = jnp.clip(1.0 + 0.18 * jax.random.normal(splits[9], (D,), jnp.float32), 0.099609375, 1.8984375).astype(jnp.bfloat16)
    latents = scatter_about(splits[10], (NLAT, D), 1.0, 6.0)
    memory_weight = scatter_about(splits[11], (D, 2 * D), D ** -0.5, 0.25)
    output_weight = scatter_about(splits[12], (D, D), D ** -0.5, 0.25)
    return {"pixels": pixels, "embed_weight": embed_weight, "level_code": level_code, "depth_kernel": depth_kernel, "norm_gain": norm_gain, "up_weight": up_weight, "up_bias": up_bias, "down_weight": down_weight, "down_bias": down_bias, "fold_gain": fold_gain, "latents": latents, "memory_weight": memory_weight, "output_weight": output_weight}


EPSILON = 1e-06

def normalize(values_in, gain):
    average = lax.optimization_barrier(jnp.mean(values_in, axis=-1, keepdims=True))
    centred = values_in - average
    spread_sq = lax.optimization_barrier(jnp.mean(centred * centred, axis=-1, keepdims=True))
    return centred * lax.rsqrt(spread_sq + EPSILON) * gain.astype(jnp.float32)

def depthwise(padded, kernel, row_count, col_count):
    conv_out = jnp.zeros((padded.shape[0], row_count, col_count, padded.shape[3]), jnp.float32)
    for row_off in range(5):
        for col_off in range(5):
            window = padded[:, row_off:row_off + row_count, col_off:col_off + col_count, :].astype(jnp.float32)
            conv_out = conv_out + window * kernel[row_off * 5 + col_off].astype(jnp.float32)
    return conv_out

def conv_block(features, padded_rows, kernel, gain, up_mat, up_shift, down_mat, down_shift):
    padded = jnp.pad(padded_rows, ((0, 0), (0, 0), (2, 2), (0, 0)))
    row_count = features.shape[1]
    col_count = features.shape[2]
    width = features.shape[3]
    conv_out = depthwise(padded, kernel, row_count, col_count)
    normed = normalize(conv_out, gain).astype(jnp.bfloat16)
    flat_rows = normed.reshape(-1, width)
    hidden = jax.nn.gelu(jnp.dot(flat_rows, up_mat, preferred_element_type=jnp.float32) + up_shift.astype(jnp.float32), approximate=False).astype(jnp.bfloat16)
    branch = jnp.dot(hidden, down_mat, preferred_element_type=jnp.float32) + down_shift.astype(jnp.float32)
    return (features.astype(jnp.float32) + branch.reshape(features.shape)).astype(jnp.bfloat16)

def embed_patches(sample_pixels, embed_weight, level_code):
    levels = sample_pixels.shape[0]
    variables = sample_pixels.shape[1]
    row_count = sample_pixels.shape[2] // PATCH
    col_count = sample_pixels.shape[3] // PATCH
    patches = sample_pixels.reshape(levels, variables, row_count, PATCH, col_count, PATCH)
    patches = patches.transpose(0, 2, 4, 1, 3, 5).reshape(levels * row_count * col_count, variables * PATCH * PATCH)
    embedded = jnp.dot(patches, embed_weight, preferred_element_type=jnp.float32).reshape(levels, row_count, col_count, -1)
    embedded = embedded + level_code[:, None, None, :].astype(jnp.float32)
    return embedded.astype(jnp.bfloat16)

def fold_levels(features, fold_gain, latents, memory_weight, output_weight):
    levels, row_count, col_count, width = features.shape
    places = row_count * col_count
    normed = normalize(features.astype(jnp.float32), fold_gain).astype(jnp.bfloat16).reshape(levels * places, width)
    keyval = jnp.dot(normed, memory_weight, preferred_element_type=jnp.float32).astype(jnp.bfloat16)
    keyval = keyval.reshape(levels, places, 2, HEADS, HSZ)
    queries = latents.reshape(NLAT, HEADS, HSZ).astype(jnp.float32)
    scores = jnp.einsum('lphe,qhe->pqlh', keyval[:, :, 0].astype(jnp.float32), queries) * HSZ ** (-0.5)
    raised = jnp.exp(scores)
    share = (raised / lax.optimization_barrier(jnp.sum(raised, axis=2, keepdims=True))).astype(jnp.bfloat16)
    mixed = jnp.einsum('pqlh,lphe->pqhe', share.astype(jnp.float32), keyval[:, :, 1].astype(jnp.float32))
    mixed = mixed.astype(jnp.bfloat16).reshape(places * NLAT, width)
    folded = jnp.dot(mixed, output_weight, preferred_element_type=jnp.float32).reshape(places, NLAT, width)
    folded = folded + latents.astype(jnp.float32)[None, :, :]
    return folded.astype(jnp.bfloat16).reshape(row_count, col_count, NLAT, width)

def reference(pixels, embed_weight, level_code, depth_kernel, norm_gain, up_weight, up_bias, down_weight, down_bias, fold_gain, latents, memory_weight, output_weight):

    def per_sample(sample_pixels):
        features = embed_patches(sample_pixels, embed_weight, level_code)
        for section_id in range(SECTIONS):
            for block_id in range(BLOCKS):
                padded_rows = jnp.pad(features, ((0, 0), (2, 2), (0, 0), (0, 0)))
                features = conv_block(features, padded_rows, depth_kernel[section_id, block_id], norm_gain[section_id, block_id], up_weight[section_id, block_id], up_bias[section_id, block_id], down_weight[section_id, block_id], down_bias[section_id, block_id])
        return fold_levels(features, fold_gain, latents, memory_weight, output_weight)
    return lax.map(per_sample, pixels)
```

```python
import functools

import jax
import jax.numpy as jnp
from jax import lax
from jax.experimental import pallas as pl
from jax.experimental.pallas import tpu as pltpu
from jax.sharding import PartitionSpec as P

HEADS = 16
HSZ = 32
PATCH = 4
NLAT = 3
BLOCKS = 2


EPSILON = 1e-06


VMEM_LIMIT = 56 * 1024 * 1024

def extended(x, sides, width):
    for axis, dim in sides:
        size, length = (lax.axis_size(axis), x.shape[dim])
        up = [(i, (i + 1) % size) for i in range(size - 1)]
        down = [(j, i) for i, j in up]
        last = lax.slice_in_dim(x, length - width, length, axis=dim)
        first = lax.slice_in_dim(x, 0, width, axis=dim)
        before = lax.ppermute(last, axis, up)
        after = lax.ppermute(first, axis, down)
        x = jnp.concatenate([before, x, after], axis=dim)
    return x


def normalize(values_in, gain):
    average = jnp.mean(values_in, axis=-1, keepdims=True)
    centred = values_in - average
    spread_sq = jnp.mean(centred * centred, axis=-1, keepdims=True)
    return centred * lax.rsqrt(spread_sq + EPSILON) * gain.astype(jnp.float32)


def depthwise(padded, kernel, row_count, col_count):
    conv_out = jnp.zeros((padded.shape[0], row_count, col_count, padded.shape[3]), jnp.float32)
    for row_off in range(5):
        for col_off in range(5):
            window = padded[
                :, row_off : row_off + row_count, col_off : col_off + col_count, :
            ].astype(jnp.float32)
            conv_out = conv_out + window * kernel[row_off * 5 + col_off].astype(jnp.float32)
    return conv_out


def conv_block(features, padded_rows, kernel, gain, up_mat, up_shift, down_mat, down_shift):
    padded = jnp.pad(padded_rows, ((0, 0), (0, 0), (2, 2), (0, 0)))
    row_count = features.shape[1]
    col_count = features.shape[2]
    width = features.shape[3]
    conv_out = depthwise(padded, kernel, row_count, col_count)
    normed = normalize(conv_out, gain).astype(jnp.bfloat16)
    flat_rows = normed.reshape(-1, width)
    hidden = jax.nn.gelu(
        jnp.dot(flat_rows, up_mat, preferred_element_type=jnp.float32)
        + up_shift.astype(jnp.float32),
        approximate=False,
    ).astype(jnp.bfloat16)
    branch = jnp.dot(hidden, down_mat, preferred_element_type=jnp.float32) + down_shift.astype(
        jnp.float32
    )
    return (features.astype(jnp.float32) + branch.reshape(features.shape)).astype(jnp.bfloat16)


def embed_patches(sample_pixels, embed_weight, level_code):
    levels = sample_pixels.shape[0]
    variables = sample_pixels.shape[1]
    row_count = sample_pixels.shape[2] // PATCH
    col_count = sample_pixels.shape[3] // PATCH
    patches = sample_pixels.reshape(levels, variables, row_count, PATCH, col_count, PATCH)
    patches = patches.transpose(0, 2, 4, 1, 3, 5).reshape(
        levels * row_count * col_count, variables * PATCH * PATCH
    )
    embedded = jnp.dot(patches, embed_weight, preferred_element_type=jnp.float32).reshape(
        levels, row_count, col_count, -1
    )
    embedded = embedded + level_code[:, None, None, :].astype(jnp.float32)
    return embedded.astype(jnp.bfloat16)


def fold_levels(features, fold_gain, latents, memory_weight, output_weight):
    levels, row_count, col_count, width = features.shape
    places = row_count * col_count
    normed = (
        normalize(features.astype(jnp.float32), fold_gain)
        .astype(jnp.bfloat16)
        .reshape(levels * places, width)
    )
    keyval = jnp.dot(normed, memory_weight, preferred_element_type=jnp.float32).astype(jnp.bfloat16)
    keyval = keyval.reshape(levels, places, 2, HEADS, HSZ)
    queries = latents.reshape(NLAT, HEADS, HSZ)
    scores = jnp.einsum(
        "lphe,qhe->pqlh", keyval[:, :, 0], queries, preferred_element_type=jnp.float32
    ) * HSZ ** (-0.5)
    raised = jnp.exp(scores)
    share = (raised / jnp.sum(raised, axis=2, keepdims=True)).astype(jnp.bfloat16)
    mixed = jnp.einsum(
        "pqlh,lphe->pqhe", share, keyval[:, :, 1], preferred_element_type=jnp.float32
    )
    mixed = mixed.astype(jnp.bfloat16).reshape(places * NLAT, width)
    folded = jnp.dot(mixed, output_weight, preferred_element_type=jnp.float32).reshape(
        places, NLAT, width
    )
    folded = folded + latents.astype(jnp.float32)[None, :, :]
    return folded.astype(jnp.bfloat16).reshape(row_count, col_count, NLAT, width)


def run_section(features, section_weights):
    for block_id in range(BLOCKS):
        padded_rows = extended(features, (("lat", 1),), 2)
        features = conv_block(
            features,
            padded_rows,
            section_weights[0][block_id],
            section_weights[1][block_id],
            section_weights[2][block_id],
            section_weights[3][block_id],
            section_weights[4][block_id],
            section_weights[5][block_id],
        )
    return features


def on_device(
    pixels,
    embed_weight,
    level_code,
    depth_kernel,
    norm_gain,
    up_weight,
    up_bias,
    down_weight,
    down_bias,
    fold_gain,
    latents,
    memory_weight,
    output_weight,
):
    segment_index = lax.axis_index("segment")
    sections = lax.axis_size("segment")
    count_all = pixels.shape[0]
    per_segment = count_all // sections

    def fold_one(features):
        return fold_levels(features, fold_gain, latents, memory_weight, output_weight)

    all_weights = (
        lax.all_gather(depth_kernel, "segment", axis=0, tiled=True),
        lax.all_gather(norm_gain, "segment", axis=0, tiled=True),
        lax.all_gather(up_weight, "segment", axis=0, tiled=True),
        lax.all_gather(up_bias, "segment", axis=0, tiled=True),
        lax.all_gather(down_weight, "segment", axis=0, tiled=True),
        lax.all_gather(down_bias, "segment", axis=0, tiled=True),
    )
    own_pixels = lax.dynamic_slice_in_dim(pixels, segment_index * per_segment, per_segment, 0)

    def per_sample(sample_pixels):
        features = embed_patches(sample_pixels, embed_weight, level_code)
        for section_id in range(sections):
            features = run_section(
                features, tuple((weight_set[section_id] for weight_set in all_weights))
            )
        return fold_one(features)

    return lax.map(per_sample, own_pixels)


def embed_kernel(ctl, pix, sel, weight, code, out):
    rows = out.shape[0]
    cols = out.shape[1]

    @pl.when(ctl[0] == 1)
    def _():
        def row(r, carry):
            spread = lax.dot_general(
                sel[...], pix[r], (((1,), (1,)), ((), ())), preferred_element_type=jnp.float32
            ).astype(jnp.bfloat16)
            total = code[...].astype(jnp.float32)
            for p in range(weight.shape[0]):
                total = total + jnp.dot(
                    spread[p * cols : (p + 1) * cols], weight[p], preferred_element_type=jnp.float32
                )
            out[r + ctl[1] * (rows - 1 - 2 * r)] = total.astype(out.dtype)
            return carry

        lax.fori_loop(0, rows, row, 0)


def stage_kernel(
    rows, paired, ctl, *refs
):
    if paired:
        x_own, x_other, *refs = refs
    else:
        x_own, *refs = refs
    (small, own_up, own_dn, oth_up, oth_dn, out, xpad, taps, ubs, cv, normed, acc, upb, dnb, sems) = refs
    width = out.shape[-1]
    hid = own_up.shape[-1]
    blocks = upb.shape[0]
    half = blocks // 2
    low = out.shape[1] // 8
    core = ctl[1]
    tile = ubs.shape[-1]

    def put(r, s, v):
        xpad[r + 2, s + 2] = v
        group = lax.broadcasted_iota(jnp.int32, v.shape, 0)
        if s >= low - 2:
            xpad[r + 2, s - (low - 2)] = jnp.where(group == 0, 0.0, pltpu.roll(v, 1, 0))
        if s < 2:
            xpad[r + 2, s + low + 2] = jnp.where(group == 7, 0.0, pltpu.roll(v, 7, 0))

    def copies(b, up, dn):
        return (
            pltpu.make_async_copy(up.at[b % half], upb.at[b], sems.at[0, b]),
            pltpu.make_async_copy(dn.at[b % half], dnb.at[b], sems.at[1, b]),
        )

    @pl.when(ctl[0] == 1)
    def _():
        for b in range(blocks):
            mine = core == b // half

            @pl.when(mine)
            def _():
                for copy in copies(b, own_up, own_dn):
                    copy.start()

            @pl.when(jnp.logical_not(mine))
            def _():
                for copy in copies(b, oth_up, oth_dn):
                    copy.start()

        zero = jnp.zeros((8, width), jnp.float32)
        for r in range(2):
            for s in range(low + 4):
                xpad[r, s] = zero

        def load_row(r, carry):
            for s in range(low):
                put(r, s, x_own[r, 8 * s : 8 * s + 8, :].astype(jnp.float32))
            return carry

        def load_other(r, carry):
            for s in range(low):
                put(rows - 1 - r, s, x_other[r, 8 * s : 8 * s + 8, :].astype(jnp.float32))
            return carry

        lax.fori_loop(0, x_own.shape[0], load_row, 0)
        if paired:
            lax.fori_loop(0, x_other.shape[0], load_other, 0)

        for b in range(blocks):
            kept = rows - 2 * (b + 1)
            sm = small[b].astype(jnp.float32)
            for i in range(5):
                for j in range(5):
                    p, q = 5 * i + j, 5 * (4 - i) + j
                    taps[p] = jnp.broadcast_to(
                        jnp.where(core == 1, sm[q : q + 1], sm[p : p + 1]), (8, width)
                    )
            gain = sm[25:26]
            for n in range(hid // tile):
                f = n * tile
                row = 26 + f // width
                ubs[n] = jnp.broadcast_to(sm[row : row + 1, f % width : f % width + tile], (8, tile))
            shift = sm[26 + hid // width : 27 + hid // width]

            def conv_rows(t, carry, gain=gain):
                for lane in range(0, width, 128):
                    lanes = slice(lane, lane + 128)
                    sums = [[None] * low for _ in range(2)]
                    for rr in range(6):
                        xs = [xpad[2 * t + rr, s, :, lanes] for s in range(low + 4)]
                        for o in range(2):
                            i = rr - o
                            if 0 <= i < 5:
                                for j in range(5):
                                    w = taps[5 * i + j, :, lanes]
                                    for s in range(low):
                                        term = xs[s + j] * w
                                        old = sums[o][s]
                                        sums[o][s] = term if old is None else old + term
                    for o in range(2):
                        for s in range(low):
                            at = (o * low + s) * 8
                            cv[at : at + 8, lanes] = sums[o][s]
                v = cv[...]
                d = v - jnp.mean(v, axis=-1, keepdims=True)
                spread = jnp.mean(d * d, axis=-1, keepdims=True)
                count = cv.shape[0]
                normed[pl.ds(pl.multiple_of(t * count, count), count), :] = (
                    d * lax.rsqrt(spread + EPSILON) * gain
                ).astype(jnp.bfloat16)
                return carry

            lax.fori_loop(0, kept // 2, conv_rows, 0)
            for copy in copies(b, own_up, own_dn):
                copy.wait()

            chunk = kept * low * 4

            def mlp(t, carry, b=b, chunk=chunk):
                at = pl.ds(pl.multiple_of(t * chunk, chunk), chunk)
                nv = normed[at, :]
                parts = []
                for n in range(hid // tile):
                    h = jnp.dot(
                        nv, upb[b, :, n * tile : (n + 1) * tile], preferred_element_type=jnp.float32
                    )
                    h = h + ubs[n, 0:1, :]
                    parts.append((0.5 * h * (1.0 + lax.erf(h * (2.0**-0.5)))).astype(jnp.bfloat16))
                acc[at, :] = jnp.dot(
                    jnp.concatenate(parts, axis=1), dnb[b], preferred_element_type=jnp.float32
                )
                return carry

            lax.fori_loop(0, 2, mlp, 0)
            final = b == blocks - 1
            turn = ctl[2]

            def update(r, carry, shift=shift, final=final, kept=kept):
                for s in range(low):
                    at = pl.ds(pl.multiple_of((r * low + s) * 8, 8), 8)
                    v = xpad[r + 2, s + 2] + acc[at, :] + shift
                    if final:
                        to = lax.rem(r + turn, kept)
                        out[to, 8 * s : 8 * s + 8, :] = v.astype(out.dtype)
                    else:
                        put(r, s, v)
                return carry

            lax.fori_loop(0, kept, update, 0)


def stage(ctl, xs, small, own_up, own_dn, oth_up, oth_dn):
    cols, width = xs[0].shape[1:]
    rows = sum(x.shape[0] for x in xs)
    blocks = small.shape[0]
    hid = own_up.shape[-1]
    kept = rows - 2 * blocks
    low = cols // 8
    tile = 256
    vmem = pl.BlockSpec(memory_space=pltpu.VMEM)
    hbm = pl.BlockSpec(memory_space=pl.ANY)
    work = (rows * blocks - blocks * (blocks + 1)) * cols
    return pl.pallas_call(
        functools.partial(stage_kernel, rows, len(xs) == 2),
        out_shape=jax.ShapeDtypeStruct((kept, cols, width), jnp.bfloat16),
        in_specs=[pl.BlockSpec(memory_space=pltpu.SMEM)] + [vmem] * (len(xs) + 1) + [hbm] * 4,
        out_specs=vmem,
        scratch_shapes=[
            pltpu.VMEM((rows + 2, low + 4, 8, width), jnp.float32),
            pltpu.VMEM((25, 8, width), jnp.float32),
            pltpu.VMEM((hid // tile, 8, tile), jnp.float32),
            pltpu.VMEM((2 * cols, width), jnp.float32),
            pltpu.VMEM((rows * cols, width), jnp.bfloat16),
            pltpu.VMEM((rows * cols, width), jnp.float32),
            pltpu.VMEM((blocks, width, hid), jnp.bfloat16),
            pltpu.VMEM((blocks, hid, width), jnp.bfloat16),
            pltpu.SemaphoreType.DMA((2, blocks)),
        ],
        compiler_params=pltpu.CompilerParams(vmem_limit_bytes=VMEM_LIMIT),
        cost_estimate=pl.CostEstimate(
            flops=8 * work * width * hid,
            bytes_accessed=4 * blocks * width * hid,
            transcendentals=work * hid,
        ),
        name="stage",
    )(ctl, *xs, small, own_up, own_dn, oth_up, oth_dn)


def embed(ctl, pix, sel, weight, code, cols):
    rows = pix.shape[0]
    width = weight.shape[-1]
    vmem = pl.BlockSpec(memory_space=pltpu.VMEM)
    return pl.pallas_call(
        embed_kernel,
        out_shape=jax.ShapeDtypeStruct((rows, cols, width), jnp.bfloat16),
        in_specs=[pl.BlockSpec(memory_space=pltpu.SMEM)] + [vmem] * 4,
        out_specs=vmem,
        cost_estimate=pl.CostEstimate(
            flops=2 * rows * cols * width * 80, bytes_accessed=2 * rows * cols * width, transcendentals=0
        ),
        name="embed",
    )(ctl, pix, sel, weight, code)


def fold_kernel(ctl, *refs):
    levels = len(refs) - 8
    xs = refs[:levels]
    gain, latents, memory_weight, output_weight, out, kv, mixed, shown = refs[levels:]
    rows, cols, width = xs[0].shape
    places = rows * cols
    low = cols // 8
    scale = HSZ**-0.5
    for i in range(levels):
        v = xs[i][...].reshape(places, width).astype(jnp.float32)
        d = v - jnp.mean(v, axis=-1, keepdims=True)
        spread = jnp.mean(d * d, axis=-1, keepdims=True)
        n = (d * lax.rsqrt(spread + EPSILON) * gain[...].astype(jnp.float32)).astype(jnp.bfloat16)
        kv[i * places : (i + 1) * places, :] = jnp.dot(
            n, memory_weight[...], preferred_element_type=jnp.float32
        ).astype(jnp.bfloat16)
    lat = latents[...].astype(jnp.float32)
    pairs = NLAT * HEADS
    at_row = lax.broadcasted_iota(jnp.int32, (pairs, width), 0)
    at_col = lax.broadcasted_iota(jnp.int32, (pairs, width), 1)
    head = at_col // HSZ == at_row % HEADS
    wide = jnp.concatenate(
        [jnp.broadcast_to(lat[q : q + 1], (HEADS, width)) for q in range(NLAT)], axis=0
    )
    queries = jnp.where(head, wide, 0.0).astype(jnp.bfloat16)
    raised = []
    for i in range(levels):
        s = lax.dot_general(
            kv[i * places : (i + 1) * places, :width],
            queries,
            (((1,), (1,)), ((), ())),
            preferred_element_type=jnp.float32,
        )
        raised.append(jnp.exp(s * scale))
    total = raised[0]
    for i in range(1, levels):
        total = total + raised[i]
    shares = [(r / total).astype(jnp.bfloat16) for r in raised]
    for q in range(NLAT):
        pick = jnp.where(jnp.logical_and(head, at_row // HEADS == q), 1.0, 0.0).astype(jnp.bfloat16)
        m = None
        for i in range(levels):
            w = jnp.dot(shares[i], pick, preferred_element_type=jnp.float32)
            term = w * kv[i * places : (i + 1) * places, width:].astype(jnp.float32)
            m = term if m is None else m + term
        mixed[q * places : (q + 1) * places, :] = m.astype(jnp.bfloat16)
    folded = jnp.dot(mixed[...], output_weight[...], preferred_element_type=jnp.float32)
    flip = ctl[0]
    for q in range(NLAT):
        for r in range(rows):
            for s in range(low):
                at = q * places + (r * low + s) * 8
                row = r + flip * (rows - 1 - 2 * r)
                start = (row * cols + s) * NLAT + q
                for lane in range(0, width, 128):
                    shown[lane // 128, pl.ds(start, 8, stride=low * NLAT), :] = (
                        folded[at : at + 8, lane : lane + 128] + lat[q : q + 1, lane : lane + 128]
                    )
    for lane in range(0, width, 128):
        out[:, lane : lane + 128] = shown[lane // 128].astype(out.dtype)


def fold(ctl, xs, gain, latents, memory_weight, output_weight):
    rows, cols, width = xs[0].shape
    places = rows * cols
    vmem = pl.BlockSpec(memory_space=pltpu.VMEM)
    return pl.pallas_call(
        fold_kernel,
        out_shape=jax.ShapeDtypeStruct((places * NLAT, width), jnp.bfloat16),
        in_specs=[pl.BlockSpec(memory_space=pltpu.SMEM)] + [vmem] * (len(xs) + 4),
        out_specs=vmem,
        scratch_shapes=[
            pltpu.VMEM((len(xs) * places, 2 * width), jnp.bfloat16),
            pltpu.VMEM((NLAT * places, width), jnp.bfloat16),
            pltpu.VMEM((width // 128, NLAT * places, 128), jnp.float32),
        ],
        cost_estimate=pl.CostEstimate(
            flops=4 * len(xs) * places * width * width, bytes_accessed=2_000_000, transcendentals=0
        ),
        name="fold",
    )(ctl, *xs, gain, latents, memory_weight, output_weight)


def fits(mesh, shapes):
    pixels, embed_weight, depth, up = shapes[0], shapes[1], shapes[3], shapes[5]
    micro, levels, _, height, wide = pixels
    lat, segment = mesh.shape["lat"], mesh.shape["segment"]
    rows, cols = height // PATCH, wide // PATCH
    blocks = depth[0] // 2 * depth[1]
    return (
        segment == 4
        and depth[0] == segment
        and micro == segment
        and micro * levels == 2 * lat
        and rows == 2 * lat
        and rows == 4 * blocks
        and cols % 32 == 0
        and wide == 128
        and lat == 2 * levels
        and up[2] % 256 == 0
        and embed_weight[1] % 256 == 0
    )


def on_columns(
    pixels,
    embed_weight,
    level_code,
    depth_kernel,
    norm_gain,
    up_weight,
    up_bias,
    down_weight,
    down_bias,
    fold_gain,
    latents,
    memory_weight,
    output_weight,
):
    seg = lax.axis_index("segment")
    place = lax.axis_index("lat")
    lat = lax.axis_size("lat")
    micro, levels, variables, height, wide = pixels.shape
    cols = wide // PATCH
    width = embed_weight.shape[1]
    far = seg // 2
    core = seg % 2
    level = place % levels
    low = cols // 8

    swap = [(0, 1), (1, 0), (2, 3), (3, 2)]
    up, dn = up_weight[0], down_weight[0]
    packed = jnp.concatenate(
        [
            depth_kernel[0],
            norm_gain[0][:, None, :],
            up_bias[0].reshape(up.shape[0], -1, width),
            down_bias[0][:, None, :],
        ],
        axis=1,
    )
    oth_packed = lax.ppermute(packed, "segment", swap)
    oth_up = lax.ppermute(up, "segment", swap)
    oth_dn = lax.ppermute(dn, "segment", swap)
    small = jnp.where(
        core == 0,
        jnp.concatenate([packed, oth_packed], axis=0),
        jnp.concatenate([oth_packed, packed], axis=0),
    )

    band = height // PATCH
    taken = pixels.reshape(2, lat, variables, band, PATCH, wide).transpose(1, 0, 3, 2, 4, 5)
    taken = taken.reshape(lat, 2, band, variables * PATCH, wide)
    got = lax.all_to_all(taken, "lat", 0, 0, tiled=True)
    images = [got[:, i].reshape(lat * band, variables * PATCH, wide) for i in range(2)]

    line = jnp.arange(wide)
    spot = line % cols
    source = ((spot % 8) * low + spot // 8) * PATCH + line // cols
    sel = (source[:, None] == line[None, :]).astype(jnp.bfloat16)
    by_col = embed_weight.reshape(variables * PATCH, PATCH, width).transpose(1, 0, 2)
    code = lax.dynamic_slice_in_dim(level_code, level, 1, 0)

    def control(on, turn):
        return jnp.stack([on, core, turn]).astype(jnp.int32)

    near_on = control(far == 0, jnp.int32(0))
    kept = 2 * band * levels // 2
    far_on = control(far == 1, lax.rem(kept - 2 * level, kept))
    weights = (small, up, dn, oth_up, oth_dn)

    onward = [(0, 2), (1, 3)]
    across = [(2, 3), (3, 2)]
    sent = []
    for i in range(2):
        e = embed(near_on, images[i], sel, by_col, code, cols)
        a = stage(near_on, (e,), *weights)
        sent.append(lax.ppermute(a, "segment", onward))
    done = []
    for i in range(2):
        other = lax.ppermute(sent[i], "segment", across)
        done.append(stage(far_on, (sent[i], other), *weights))
    home = lax.ppermute(done[0], "segment", [(j, i) for i, j in onward])
    whole = jnp.where(far == 0, home, done[1])

    pieces = []
    for t in range(levels):
        pairs = []
        for s in range(4):
            for l in range(lat):
                k = (l % levels + t) % levels
                to_lat = k if s % 2 == 0 else lat - 1 - k
                to_seg = 2 * (s // 2) + l // levels
                pairs.append((s * lat + l, to_seg * lat + to_lat))
        pieces.append(lax.ppermute(whole[2 * t : 2 * t + 2], ("segment", "lat"), pairs))
    flip = (place >= levels).astype(jnp.int32).reshape(1)
    folded = fold(flip, pieces, fold_gain[None, :], latents, memory_weight, output_weight)
    return folded.reshape(1, band, cols, NLAT, width)


def solution(mesh):
    specs = (
        P(None, None, None, "lat", None),
        P(),
        P(),
        P("segment", None, None, None),
        P("segment", None, None),
        P("segment", None, None, None),
        P("segment", None, None),
        P("segment", None, None, None),
        P("segment", None, None),
        P(),
        P(),
        P(),
        P(),
    )

    def program(*arrays):
        body = on_columns if fits(mesh, [a.shape for a in arrays]) else on_device
        return jax.shard_map(
            body,
            mesh=mesh,
            in_specs=specs,
            out_specs=P("segment", "lat", None, None, None),
            check_vma=False,
        )(*arrays)

    return program
```

```python
import functools

import jax
import jax.numpy as jnp
from jax import lax
from jax.experimental import pallas as pl
from jax.experimental.pallas import tpu as pltpu
from jax.sharding import PartitionSpec as P

HEADS = 16
HSZ = 32
PATCH = 4
NLAT = 3
BLOCKS = 2


EPSILON = 1e-06


VMEM_LIMIT = 32 * 1024 * 1024
GROUP = 16
UNROLL = 4

def extended(x, sides, width):
    for axis, dim in sides:
        size, length = (lax.axis_size(axis), x.shape[dim])
        up = [(i, (i + 1) % size) for i in range(size - 1)]
        down = [(j, i) for i, j in up]
        last = lax.slice_in_dim(x, length - width, length, axis=dim)
        first = lax.slice_in_dim(x, 0, width, axis=dim)
        before = lax.ppermute(last, axis, up)
        after = lax.ppermute(first, axis, down)
        x = jnp.concatenate([before, x, after], axis=dim)
    return x


def normalize(values_in, gain):
    average = jnp.mean(values_in, axis=-1, keepdims=True)
    centred = values_in - average
    spread_sq = jnp.mean(centred * centred, axis=-1, keepdims=True)
    return centred * lax.rsqrt(spread_sq + EPSILON) * gain.astype(jnp.float32)


def depthwise(padded, kernel, row_count, col_count):
    conv_out = jnp.zeros((padded.shape[0], row_count, col_count, padded.shape[3]), jnp.float32)
    for row_off in range(5):
        for col_off in range(5):
            window = padded[
                :, row_off : row_off + row_count, col_off : col_off + col_count, :
            ].astype(jnp.float32)
            conv_out = conv_out + window * kernel[row_off * 5 + col_off].astype(jnp.float32)
    return conv_out


def conv_block(features, padded_rows, kernel, gain, up_mat, up_shift, down_mat, down_shift):
    padded = jnp.pad(padded_rows, ((0, 0), (0, 0), (2, 2), (0, 0)))
    row_count = features.shape[1]
    col_count = features.shape[2]
    width = features.shape[3]
    conv_out = depthwise(padded, kernel, row_count, col_count)
    normed = normalize(conv_out, gain).astype(jnp.bfloat16)
    flat_rows = normed.reshape(-1, width)
    hidden = jax.nn.gelu(
        jnp.dot(flat_rows, up_mat, preferred_element_type=jnp.float32)
        + up_shift.astype(jnp.float32),
        approximate=False,
    ).astype(jnp.bfloat16)
    branch = jnp.dot(hidden, down_mat, preferred_element_type=jnp.float32) + down_shift.astype(
        jnp.float32
    )
    return (features.astype(jnp.float32) + branch.reshape(features.shape)).astype(jnp.bfloat16)


def embed_patches(sample_pixels, embed_weight, level_code):
    levels = sample_pixels.shape[0]
    variables = sample_pixels.shape[1]
    row_count = sample_pixels.shape[2] // PATCH
    col_count = sample_pixels.shape[3] // PATCH
    patches = sample_pixels.reshape(levels, variables, row_count, PATCH, col_count, PATCH)
    patches = patches.transpose(0, 2, 4, 1, 3, 5).reshape(
        levels * row_count * col_count, variables * PATCH * PATCH
    )
    embedded = jnp.dot(patches, embed_weight, preferred_element_type=jnp.float32).reshape(
        levels, row_count, col_count, -1
    )
    embedded = embedded + level_code[:, None, None, :].astype(jnp.float32)
    return embedded.astype(jnp.bfloat16)


def fold_levels(features, fold_gain, latents, memory_weight, output_weight):
    levels, row_count, col_count, width = features.shape
    places = row_count * col_count
    normed = (
        normalize(features.astype(jnp.float32), fold_gain)
        .astype(jnp.bfloat16)
        .reshape(levels * places, width)
    )
    keyval = jnp.dot(normed, memory_weight, preferred_element_type=jnp.float32).astype(jnp.bfloat16)
    keyval = keyval.reshape(levels, places, 2, HEADS, HSZ)
    queries = latents.reshape(NLAT, HEADS, HSZ)
    scores = jnp.einsum(
        "lphe,qhe->pqlh", keyval[:, :, 0], queries, preferred_element_type=jnp.float32
    ) * HSZ ** (-0.5)
    raised = jnp.exp(scores)
    share = (raised / jnp.sum(raised, axis=2, keepdims=True)).astype(jnp.bfloat16)
    mixed = jnp.einsum(
        "pqlh,lphe->pqhe", share, keyval[:, :, 1], preferred_element_type=jnp.float32
    )
    mixed = mixed.astype(jnp.bfloat16).reshape(places * NLAT, width)
    folded = jnp.dot(mixed, output_weight, preferred_element_type=jnp.float32).reshape(
        places, NLAT, width
    )
    folded = folded + latents.astype(jnp.float32)[None, :, :]
    return folded.astype(jnp.bfloat16).reshape(row_count, col_count, NLAT, width)


def run_section(features, section_weights):
    for block_id in range(BLOCKS):
        padded_rows = extended(features, (("lat", 1),), 2)
        features = conv_block(
            features,
            padded_rows,
            section_weights[0][block_id],
            section_weights[1][block_id],
            section_weights[2][block_id],
            section_weights[3][block_id],
            section_weights[4][block_id],
            section_weights[5][block_id],
        )
    return features


def on_device(
    pixels,
    embed_weight,
    level_code,
    depth_kernel,
    norm_gain,
    up_weight,
    up_bias,
    down_weight,
    down_bias,
    fold_gain,
    latents,
    memory_weight,
    output_weight,
):
    segment_index = lax.axis_index("segment")
    sections = lax.axis_size("segment")
    count_all = pixels.shape[0]
    per_segment = count_all // sections

    def fold_one(features):
        return fold_levels(features, fold_gain, latents, memory_weight, output_weight)

    all_weights = (
        lax.all_gather(depth_kernel, "segment", axis=0, tiled=True),
        lax.all_gather(norm_gain, "segment", axis=0, tiled=True),
        lax.all_gather(up_weight, "segment", axis=0, tiled=True),
        lax.all_gather(up_bias, "segment", axis=0, tiled=True),
        lax.all_gather(down_weight, "segment", axis=0, tiled=True),
        lax.all_gather(down_bias, "segment", axis=0, tiled=True),
    )
    own_pixels = lax.dynamic_slice_in_dim(pixels, segment_index * per_segment, per_segment, 0)

    def per_sample(sample_pixels):
        features = embed_patches(sample_pixels, embed_weight, level_code)
        for section_id in range(sections):
            features = run_section(
                features, tuple((weight_set[section_id] for weight_set in all_weights))
            )
        return fold_one(features)

    return lax.map(per_sample, own_pixels)


def spread_pixels(pix, weight, code, level, spread, by_col):
    bands, variables, lines, wide = pix.shape
    cols = wide // PATCH
    low = cols // GROUP
    taken = variables * lines
    line = lax.broadcasted_iota(jnp.int32, (wide, wide), 0)
    source = ((line % GROUP) * low + (line % cols) // GROUP) * PATCH + line // cols
    pick = jnp.where(source == lax.broadcasted_iota(jnp.int32, (wide, wide), 1), 1.0, 0.0)
    pick = pick.astype(jnp.bfloat16)
    for n in range(bands):
        part = lax.dot_general(
            pick,
            pix[n].reshape(taken, wide),
            (((1,), (1,)), ((), ())),
            preferred_element_type=jnp.float32,
        ).astype(jnp.bfloat16)
        for p in range(PATCH):
            spread[p, n * cols : (n + 1) * cols, :] = part[p * cols : (p + 1) * cols]
    depth = weight.shape[0]
    to = lax.broadcasted_iota(jnp.int32, (taken, depth), 0)
    at = lax.broadcasted_iota(jnp.int32, (taken, depth), 1)
    shown = code[0:1, :].astype(jnp.float32)
    for n in range(1, code.shape[0]):
        shown = jnp.where(level == n, code[n : n + 1, :].astype(jnp.float32), shown)
    rows = []
    for b in range(lines // PATCH):
        total = jnp.broadcast_to(shown, (bands * cols, shown.shape[1]))
        for p in range(PATCH):
            base = (to // lines) * (PATCH * PATCH) + (to % PATCH) * PATCH + p
            same = jnp.logical_and(base == at, (to % lines) // PATCH == b)
            by_col[...] = jnp.dot(
                jnp.where(same, 1.0, 0.0).astype(jnp.bfloat16),
                weight[...],
                preferred_element_type=jnp.float32,
            ).astype(jnp.bfloat16)
            total = total + jnp.dot(spread[p], by_col[...], preferred_element_type=jnp.float32)
        rows.append(total)
    return rows


def stage_kernel(rows, near, *refs):
    if near:
        pix, embed_weight, level_code, *refs = refs
    else:
        x_own, x_other, *refs = refs
    (
        own_depth, own_gain, own_ub, own_db, oth_depth, oth_gain, oth_ub, oth_db,
        own_up, own_dn, oth_up, oth_dn, out,
        xpad, taps, ubs, normed, acc, upb, dnb, sems, *scratch,
    ) = refs
    segment = lax.axis_index("segment")
    place = lax.axis_index("lat")
    width = out.shape[-1]
    hid = own_up.shape[-1]
    blocks = upb.shape[0]
    half = blocks // 2
    low = out.shape[1] // GROUP
    core = lax.rem(segment, 2)
    level = lax.rem(place, out.shape[0] // 2)
    tile = ubs.shape[-1]
    chunks = width // 128


    def put(r, s, v):
        xpad[r + 2, s + 2] = v.astype(xpad.dtype)
        group = lax.broadcasted_iota(jnp.int32, v.shape, 0)
        for d in (-2, -1, low, low + 1):
            if d % low == s:
                by = -(d // low)
                edge = 0 if by > 0 else GROUP - 1
                moved = jnp.where(group == edge, 0.0, pltpu.roll(v, by % GROUP, 0))
                xpad[r + 2, d + 2] = moved.astype(xpad.dtype)

    def copies(b, up, dn):
        return (
            pltpu.make_async_copy(up.at[b % half], upb.at[b], sems.at[0, b]),
            pltpu.make_async_copy(dn.at[b % half], dnb.at[b], sems.at[1, b]),
        )

    @pl.when(segment // 2 == (0 if near else 1))
    def _():
        for b in range(blocks):
            mine = core == b // half

            @pl.when(mine)
            def _():
                for copy in copies(b, own_up, own_dn):
                    copy.start()

            @pl.when(jnp.logical_not(mine))
            def _():
                for copy in copies(b, oth_up, oth_dn):
                    copy.start()

        zero = jnp.zeros((GROUP, width), xpad.dtype)
        for r in range(2):
            for s in range(low + 4):
                xpad[r, s] = zero

        def load_row(r, carry):
            for s in range(low):
                put(r, s, x_own[r, GROUP * s : GROUP * (s + 1), :].astype(jnp.float32))
            return carry

        def load_other(r, carry):
            for s in range(low):
                put(rows - 1 - r, s, x_other[r, GROUP * s : GROUP * (s + 1), :].astype(jnp.float32))
            return carry

        if near:
            cols = GROUP * low
            totals = spread_pixels(pix, embed_weight, level_code, level, *scratch)
            for n in range(rows):
                total = totals[n % len(totals)]
                to = n + core * (rows - 1 - 2 * n)
                for s in range(low):
                    at = (n // len(totals)) * cols + GROUP * s
                    put(to, s, total[at : at + GROUP])
        else:
            lax.fori_loop(0, x_own.shape[0], load_row, 0)
            lax.fori_loop(0, x_other.shape[0], load_other, 0)

        for b in range(blocks):
            kept = rows - 2 * (b + 1)
            def chosen(own, oth, *at):
                even, odd = (own, oth) if b < half else (oth, own)
                return jnp.where(
                    core == 1, odd[at].astype(jnp.float32), even[at].astype(jnp.float32)
                )

            k = b % half
            even, odd = (own_depth, oth_depth) if b < half else (oth_depth, own_depth)
            for i in range(5):
                for j in range(5):
                    p, q = 5 * i + j, 5 * (4 - i) + j
                    tap = jnp.where(
                        core == 1,
                        odd[q, k : k + 1, :].astype(jnp.float32),
                        even[p, k : k + 1, :].astype(jnp.float32),
                    )
                    taps[p] = jnp.broadcast_to(tap, (8, width))
            line = slice(k, k + 1)
            gain = chosen(own_gain, oth_gain, line, slice(None))
            shift = chosen(own_db, oth_db, line, slice(None))
            ub = chosen(own_ub, oth_ub, line, slice(None))
            for n in range(hid // tile):
                ubs[n] = jnp.broadcast_to(ub[:, n * tile : (n + 1) * tile], (8, tile))

            def conv_rows(n, carry):
                t = n // chunks
                lanes = pl.ds(pl.multiple_of((n % chunks) * 128, 128), 128)
                sums = [[None] * low for _ in range(2)]

                def line(r):
                    return [
                        xpad[2 * t + r, s, :, lanes].astype(jnp.bfloat16) for s in range(low + 4)
                    ]

                window = [line(0)]
                for i in range(5):
                    window = [*window[-1:], line(i + 1)]
                    tap = []
                    for j in range(5):
                        w = taps[5 * i + j, :, lanes]
                        tap.append(jnp.concatenate([w, w], axis=0).astype(jnp.bfloat16))
                    for o in range(2):
                        for s in range(low):
                            part = window[o][s] * tap[0]
                            for j in range(1, 5):
                                part = part + window[o][s + j] * tap[j]
                            sums[o][s] = part if i == 0 else sums[o][s] + part
                for o in range(2):
                    for s in range(low):
                        at = pl.multiple_of(((2 * t + o) * low + s) * GROUP, GROUP)
                        acc[pl.ds(at, GROUP), lanes] = sums[o][s].astype(jnp.float32)
                return carry

            lax.fori_loop(0, kept // 2 * chunks, conv_rows, 0, unroll=UNROLL)
            part = kept * low * GROUP // 2

            def norm_rows(t, gain=gain, part=part):
                at = pl.ds(pl.multiple_of(t * part, part), part)
                v = acc[at, :]
                d = v - jnp.mean(v, axis=-1, keepdims=True)
                spread = jnp.mean(d * d, axis=-1, keepdims=True)
                normed[at, :] = (d * lax.rsqrt(spread + EPSILON) * gain).astype(jnp.bfloat16)

            norm_rows(0)
            for copy in copies(b, own_up, own_dn):
                copy.wait()

            def mlp(t, carry, b=b, part=part):
                at = pl.ds(pl.multiple_of(t * part, part), part)
                nv = normed[at, :]
                if t == 0:
                    norm_rows(1)
                parts = []
                for n in range(hid // tile):
                    h = jnp.dot(
                        nv, upb[b, :, n * tile : (n + 1) * tile], preferred_element_type=jnp.float32
                    )
                    h = h + ubs[n, 0:1, :]
                    parts.append((0.5 * h * (1.0 + lax.erf(h * (2.0**-0.5)))).astype(jnp.bfloat16))
                acc[at, :] = jnp.dot(
                    jnp.concatenate(parts, axis=1), dnb[b], preferred_element_type=jnp.float32
                )
                return carry

            mlp(0, 0)
            mlp(1, 0)
            final = b == blocks - 1
            turn = 0 if near else kept - 2 * level

            def update(r, carry, shift=shift, final=final, kept=kept, turn=turn):
                for s in range(low):
                    at = pl.ds(pl.multiple_of((r * low + s) * GROUP, GROUP), GROUP)
                    v = xpad[r + 2, s + 2] + acc[at, :] + shift
                    if final:
                        to = lax.rem(r + turn, kept)
                        out[to, GROUP * s : GROUP * (s + 1), :] = v.astype(out.dtype)
                    else:
                        put(r, s, v)
                return carry

            lax.fori_loop(0, kept, update, 0)


def placed(x):
    return pltpu.with_memory_space_constraint(x, pltpu.VMEM)


def stage(near, xs, cols, width, smalls, own_up, own_dn, oth_up, oth_dn):
    rows = 2 * xs[0].shape[0]
    blocks = 2 * own_up.shape[0]
    hid = own_up.shape[-1]
    kept = rows - 2 * blocks
    low = cols // GROUP
    tile = 256
    vmem = pl.BlockSpec(memory_space=pltpu.VMEM)
    hbm = pl.BlockSpec(memory_space=pltpu.HBM)
    work = (rows * blocks - blocks * (blocks + 1)) * cols
    scratch = [
        pltpu.VMEM((rows + 2, low + 4, GROUP, width), jnp.float32),
        pltpu.VMEM((25, 8, width), jnp.float32),
        pltpu.VMEM((hid // tile, 8, tile), jnp.float32),
        pltpu.VMEM((rows * cols, width), jnp.bfloat16),
        pltpu.VMEM((rows * cols, width), jnp.float32),
        pltpu.VMEM((blocks, width, hid), jnp.bfloat16),
        pltpu.VMEM((blocks, hid, width), jnp.bfloat16),
        pltpu.SemaphoreType.DMA((2, blocks)),
    ]
    if near:
        bands, variables, lines, _ = xs[0].shape
        scratch += [
            pltpu.VMEM((PATCH, bands * cols, variables * lines), jnp.bfloat16),
            pltpu.VMEM((variables * lines, width), jnp.bfloat16),
        ]
    return pl.pallas_call(
        functools.partial(stage_kernel, rows, near),
        out_shape=pltpu.VMEM((kept, cols, width), jnp.bfloat16),
        in_specs=[vmem] * (len(xs) + len(smalls)) + [hbm] * 2 + [vmem] * 2,
        out_specs=vmem,
        scratch_shapes=scratch,
        compiler_params=pltpu.CompilerParams(vmem_limit_bytes=VMEM_LIMIT),
        cost_estimate=pl.CostEstimate(
            flops=8 * work * width * hid,
            bytes_accessed=4 * blocks * width * hid,
            transcendentals=work * hid,
        ),
        name="near_stage" if near else "far_stage",
    )(*(placed(x) for x in xs[:1]), *(xs[1:] if near else (placed(xs[1]),)), *smalls[:4],
      *(placed(w) for w in smalls[4:]), own_up, own_dn, placed(oth_up), placed(oth_dn))


def fold_kernel(*refs):
    levels = len(refs) - 8
    xs = refs[:levels]
    gain, latents, memory_weight, output_weight, out, kv, mixed, shown = refs[levels:]
    rows, cols, width = xs[0].shape
    places = rows * cols
    low = cols // GROUP
    scale = HSZ**-0.5
    for i in range(levels):
        v = xs[i][...].reshape(places, width).astype(jnp.float32)
        d = v - jnp.mean(v, axis=-1, keepdims=True)
        spread = jnp.mean(d * d, axis=-1, keepdims=True)
        n = (d * lax.rsqrt(spread + EPSILON) * gain[...].astype(jnp.float32)).astype(jnp.bfloat16)
        kv[i * places : (i + 1) * places, :] = jnp.dot(
            n, memory_weight[...], preferred_element_type=jnp.float32
        ).astype(jnp.bfloat16)
    lat = latents[...].astype(jnp.float32)
    pairs = NLAT * HEADS
    at_row = lax.broadcasted_iota(jnp.int32, (pairs, width), 0)
    at_col = lax.broadcasted_iota(jnp.int32, (pairs, width), 1)
    head = at_col // HSZ == at_row % HEADS
    wide = jnp.concatenate(
        [jnp.broadcast_to(lat[q : q + 1], (HEADS, width)) for q in range(NLAT)], axis=0
    )
    queries = jnp.where(head, wide, 0.0).astype(jnp.bfloat16)
    raised = []
    for i in range(levels):
        s = lax.dot_general(
            kv[i * places : (i + 1) * places, :width],
            queries,
            (((1,), (1,)), ((), ())),
            preferred_element_type=jnp.float32,
        )
        raised.append(jnp.exp(s * scale))
    total = raised[0]
    for i in range(1, levels):
        total = total + raised[i]
    shares = [(r / total).astype(jnp.bfloat16) for r in raised]
    for q in range(NLAT):
        pick = jnp.where(jnp.logical_and(head, at_row // HEADS == q), 1.0, 0.0).astype(jnp.bfloat16)
        m = None
        for i in range(levels):
            w = jnp.dot(shares[i], pick, preferred_element_type=jnp.float32)
            term = w * kv[i * places : (i + 1) * places, width:].astype(jnp.float32)
            m = term if m is None else m + term
        mixed[q * places : (q + 1) * places, :] = m.astype(jnp.bfloat16)
    folded = jnp.dot(mixed[...], output_weight[...], preferred_element_type=jnp.float32)
    flip = (lax.axis_index("lat") >= levels).astype(jnp.int32)
    for q in range(NLAT):
        for r in range(rows):
            for s in range(cols // 8):
                at = q * places + r * cols + 8 * s
                row = r + flip * (rows - 1 - 2 * r)
                group, first = divmod(8 * s, GROUP)
                start = (row * NLAT + q) * cols + first * low + group
                for lane in range(0, width, 128):
                    shown[lane // 128, pl.ds(start, 8, stride=low), :] = (
                        folded[at : at + 8, lane : lane + 128] + lat[q : q + 1, lane : lane + 128]
                    )
    for lane in range(0, width, 128):
        v = shown[lane // 128].astype(out.dtype)
        out[:, :, :, lane : lane + 128] = v.reshape(rows, NLAT, cols, 128)


def fold(xs, gain, latents, memory_weight, output_weight):
    rows, cols, width = xs[0].shape
    places = rows * cols
    vmem = pl.BlockSpec(memory_space=pltpu.VMEM)
    return pl.pallas_call(
        fold_kernel,
        out_shape=jax.ShapeDtypeStruct((rows, NLAT, cols, width), jnp.bfloat16),
        in_specs=[vmem] * (len(xs) + 4),
        out_specs=vmem,
        scratch_shapes=[
            pltpu.VMEM((len(xs) * places, 2 * width), jnp.bfloat16),
            pltpu.VMEM((NLAT * places, width), jnp.bfloat16),
            pltpu.VMEM((width // 128, NLAT * places, 128), jnp.float32),
        ],
        cost_estimate=pl.CostEstimate(
            flops=4 * len(xs) * places * width * width, bytes_accessed=2_000_000, transcendentals=0
        ),
        name="fold",
    )(
        *(placed(x) for x in (*xs, gain, latents, memory_weight, output_weight))
    )


def fits(mesh, shapes):
    pixels, embed_weight, depth, up = shapes[0], shapes[1], shapes[3], shapes[5]
    micro, levels, _, height, wide = pixels
    lat, segment = mesh.shape["lat"], mesh.shape["segment"]
    rows, cols = height // PATCH, wide // PATCH
    blocks = depth[0] // 2 * depth[1]
    return (
        segment == 4
        and depth[0] == segment
        and micro == segment
        and micro * levels == 2 * lat
        and rows == 2 * lat
        and rows == 4 * blocks
        and cols % 32 == 0
        and wide == 128
        and lat == 2 * levels
        and up[2] % 256 == 0
        and embed_weight[1] % 256 == 0
    )


def on_columns(
    pixels,
    embed_weight,
    level_code,
    depth_kernel,
    norm_gain,
    up_weight,
    up_bias,
    down_weight,
    down_bias,
    fold_gain,
    latents,
    memory_weight,
    output_weight,
):
    seg = lax.axis_index("segment")
    lat = lax.axis_size("lat")
    micro, levels, variables, height, wide = pixels.shape
    cols = wide // PATCH
    width = embed_weight.shape[1]
    far = seg // 2

    swap = [(0, 1), (1, 0), (2, 3), (3, 2)]
    own = (depth_kernel[0].transpose(1, 0, 2), norm_gain[0], up_bias[0], down_bias[0])
    own_up, own_dn = up_weight[0], down_weight[0]
    oth = tuple(lax.ppermute(w, "segment", swap) for w in own)
    oth_up = lax.ppermute(own_up, "segment", swap)
    oth_dn = lax.ppermute(own_dn, "segment", swap)
    weights = (own + oth, own_up, own_dn, oth_up, oth_dn)

    got = lax.all_to_all(
        pixels.reshape(2, lat, variables, height, wide), "lat", 1, 1, tiled=True
    )

    onward = [(0, 2), (1, 3)]
    across = [(2, 3), (3, 2)]
    sent = []
    for i in range(2):
        a = stage(True, (got[i], embed_weight, level_code), cols, width, *weights)
        if i:
            a, sent[0] = lax.optimization_barrier((a, sent[0]))
        sent.append(lax.ppermute(a, "segment", onward))
    done = []
    for i in range(2):
        if i:
            done[0], sent[i] = lax.optimization_barrier((done[0], sent[i]))
        other = lax.ppermute(sent[i], "segment", across)
        done.append(stage(False, (sent[i], other), cols, width, *weights))
    home = lax.ppermute(done[0], "segment", [(j, i) for i, j in onward])

    pieces = []
    for t in range(levels):
        pairs = []
        for s in range(4):
            for l in range(lat):
                k = (l % levels + t) % levels
                to_lat = k if s % 2 == 0 else lat - 1 - k
                to_seg = 2 * (s // 2) + l // levels
                pairs.append((s * lat + l, to_seg * lat + to_lat))
        piece = jnp.where(far == 0, home[2 * t : 2 * t + 2], done[1][2 * t : 2 * t + 2])
        pieces.append(lax.ppermute(piece, ("segment", "lat"), pairs))
    folded = fold(pieces, fold_gain[None, :], latents, memory_weight, output_weight)
    return folded.transpose(0, 2, 1, 3)[None]


def solution(mesh):
    specs = (
        P(None, None, None, "lat", None),
        P(),
        P(),
        P("segment", None, None, None),
        P("segment", None, None),
        P("segment", None, None, None),
        P("segment", None, None),
        P("segment", None, None, None),
        P("segment", None, None),
        P(),
        P(),
        P(),
        P(),
    )

    def program(*arrays):
        body = on_columns if fits(mesh, [a.shape for a in arrays]) else on_device
        return jax.shard_map(
            body,
            mesh=mesh,
            in_specs=specs,
            out_specs=P("segment", "lat", None, None, None),
            check_vma=False,
        )(*arrays)

    return program
```

```python
import functools

import jax
import jax.numpy as jnp
from jax import lax
from jax.experimental import pallas as pl
from jax.experimental.pallas import tpu as pltpu
from jax.sharding import PartitionSpec as P

HEADS = 16
HSZ = 32
PATCH = 4
NLAT = 3
BLOCKS = 2


EPSILON = 1e-06


VMEM_LIMIT = 32 * 1024 * 1024
GROUP = 16
UNROLL = 4

def extended(x, sides, width):
    for axis, dim in sides:
        size, length = (lax.axis_size(axis), x.shape[dim])
        up = [(i, (i + 1) % size) for i in range(size - 1)]
        down = [(j, i) for i, j in up]
        last = lax.slice_in_dim(x, length - width, length, axis=dim)
        first = lax.slice_in_dim(x, 0, width, axis=dim)
        before = lax.ppermute(last, axis, up)
        after = lax.ppermute(first, axis, down)
        x = jnp.concatenate([before, x, after], axis=dim)
    return x


def normalize(values_in, gain):
    average = jnp.mean(values_in, axis=-1, keepdims=True)
    centred = values_in - average
    spread_sq = jnp.mean(centred * centred, axis=-1, keepdims=True)
    return centred * lax.rsqrt(spread_sq + EPSILON) * gain.astype(jnp.float32)


def depthwise(padded, kernel, row_count, col_count):
    conv_out = jnp.zeros((padded.shape[0], row_count, col_count, padded.shape[3]), jnp.float32)
    for row_off in range(5):
        for col_off in range(5):
            window = padded[
                :, row_off : row_off + row_count, col_off : col_off + col_count, :
            ].astype(jnp.float32)
            conv_out = conv_out + window * kernel[row_off * 5 + col_off].astype(jnp.float32)
    return conv_out


def conv_block(features, padded_rows, kernel, gain, up_mat, up_shift, down_mat, down_shift):
    padded = jnp.pad(padded_rows, ((0, 0), (0, 0), (2, 2), (0, 0)))
    row_count = features.shape[1]
    col_count = features.shape[2]
    width = features.shape[3]
    conv_out = depthwise(padded, kernel, row_count, col_count)
    normed = normalize(conv_out, gain).astype(jnp.bfloat16)
    flat_rows = normed.reshape(-1, width)
    hidden = jax.nn.gelu(
        jnp.dot(flat_rows, up_mat, preferred_element_type=jnp.float32)
        + up_shift.astype(jnp.float32),
        approximate=False,
    ).astype(jnp.bfloat16)
    branch = jnp.dot(hidden, down_mat, preferred_element_type=jnp.float32) + down_shift.astype(
        jnp.float32
    )
    return (features.astype(jnp.float32) + branch.reshape(features.shape)).astype(jnp.bfloat16)


def embed_patches(sample_pixels, embed_weight, level_code):
    levels = sample_pixels.shape[0]
    variables = sample_pixels.shape[1]
    row_count = sample_pixels.shape[2] // PATCH
    col_count = sample_pixels.shape[3] // PATCH
    patches = sample_pixels.reshape(levels, variables, row_count, PATCH, col_count, PATCH)
    patches = patches.transpose(0, 2, 4, 1, 3, 5).reshape(
        levels * row_count * col_count, variables * PATCH * PATCH
    )
    embedded = jnp.dot(patches, embed_weight, preferred_element_type=jnp.float32).reshape(
        levels, row_count, col_count, -1
    )
    embedded = embedded + level_code[:, None, None, :].astype(jnp.float32)
    return embedded.astype(jnp.bfloat16)


def fold_levels(features, fold_gain, latents, memory_weight, output_weight):
    levels, row_count, col_count, width = features.shape
    places = row_count * col_count
    normed = (
        normalize(features.astype(jnp.float32), fold_gain)
        .astype(jnp.bfloat16)
        .reshape(levels * places, width)
    )
    keyval = jnp.dot(normed, memory_weight, preferred_element_type=jnp.float32).astype(jnp.bfloat16)
    keyval = keyval.reshape(levels, places, 2, HEADS, HSZ)
    queries = latents.reshape(NLAT, HEADS, HSZ)
    scores = jnp.einsum(
        "lphe,qhe->pqlh", keyval[:, :, 0], queries, preferred_element_type=jnp.float32
    ) * HSZ ** (-0.5)
    raised = jnp.exp(scores)
    share = (raised / jnp.sum(raised, axis=2, keepdims=True)).astype(jnp.bfloat16)
    mixed = jnp.einsum(
        "pqlh,lphe->pqhe", share, keyval[:, :, 1], preferred_element_type=jnp.float32
    )
    mixed = mixed.astype(jnp.bfloat16).reshape(places * NLAT, width)
    folded = jnp.dot(mixed, output_weight, preferred_element_type=jnp.float32).reshape(
        places, NLAT, width
    )
    folded = folded + latents.astype(jnp.float32)[None, :, :]
    return folded.astype(jnp.bfloat16).reshape(row_count, col_count, NLAT, width)


def run_section(features, section_weights):
    for block_id in range(BLOCKS):
        padded_rows = extended(features, (("lat", 1),), 2)
        features = conv_block(
            features,
            padded_rows,
            section_weights[0][block_id],
            section_weights[1][block_id],
            section_weights[2][block_id],
            section_weights[3][block_id],
            section_weights[4][block_id],
            section_weights[5][block_id],
        )
    return features


def on_device(
    pixels,
    embed_weight,
    level_code,
    depth_kernel,
    norm_gain,
    up_weight,
    up_bias,
    down_weight,
    down_bias,
    fold_gain,
    latents,
    memory_weight,
    output_weight,
):
    segment_index = lax.axis_index("segment")
    sections = lax.axis_size("segment")
    count_all = pixels.shape[0]
    per_segment = count_all // sections

    def fold_one(features):
        return fold_levels(features, fold_gain, latents, memory_weight, output_weight)

    all_weights = (
        lax.all_gather(depth_kernel, "segment", axis=0, tiled=True),
        lax.all_gather(norm_gain, "segment", axis=0, tiled=True),
        lax.all_gather(up_weight, "segment", axis=0, tiled=True),
        lax.all_gather(up_bias, "segment", axis=0, tiled=True),
        lax.all_gather(down_weight, "segment", axis=0, tiled=True),
        lax.all_gather(down_bias, "segment", axis=0, tiled=True),
    )
    own_pixels = lax.dynamic_slice_in_dim(pixels, segment_index * per_segment, per_segment, 0)

    def per_sample(sample_pixels):
        features = embed_patches(sample_pixels, embed_weight, level_code)
        for section_id in range(sections):
            features = run_section(
                features, tuple((weight_set[section_id] for weight_set in all_weights))
            )
        return fold_one(features)

    return lax.map(per_sample, own_pixels)


def spread_pixels(pix, weight, code, level, spread, by_col):
    bands, variables, lines, wide = pix.shape
    cols = wide // PATCH
    low = cols // GROUP
    taken = variables * lines
    line = lax.broadcasted_iota(jnp.int32, (wide, wide), 0)
    source = ((line % GROUP) * low + (line % cols) // GROUP) * PATCH + line // cols
    pick = jnp.where(source == lax.broadcasted_iota(jnp.int32, (wide, wide), 1), 1.0, 0.0)
    pick = pick.astype(jnp.bfloat16)
    for n in range(bands):
        part = lax.dot_general(
            pick,
            pix[n].reshape(taken, wide),
            (((1,), (1,)), ((), ())),
            preferred_element_type=jnp.float32,
        ).astype(jnp.bfloat16)
        for p in range(PATCH):
            spread[p, n * cols : (n + 1) * cols, :] = part[p * cols : (p + 1) * cols]
    depth = weight.shape[0]
    to = lax.broadcasted_iota(jnp.int32, (taken, depth), 0)
    at = lax.broadcasted_iota(jnp.int32, (taken, depth), 1)
    shown = code[0:1, :].astype(jnp.float32)
    for n in range(1, code.shape[0]):
        shown = jnp.where(level == n, code[n : n + 1, :].astype(jnp.float32), shown)
    rows = []
    for b in range(lines // PATCH):
        total = jnp.broadcast_to(shown, (bands * cols, shown.shape[1]))
        for p in range(PATCH):
            base = (to // lines) * (PATCH * PATCH) + (to % PATCH) * PATCH + p
            same = jnp.logical_and(base == at, (to % lines) // PATCH == b)
            by_col[...] = jnp.dot(
                jnp.where(same, 1.0, 0.0).astype(jnp.bfloat16),
                weight[...],
                preferred_element_type=jnp.float32,
            ).astype(jnp.bfloat16)
            total = total + jnp.dot(spread[p], by_col[...], preferred_element_type=jnp.float32)
        rows.append(total)
    return rows


def stage_kernel(rows, near, *refs):
    if near:
        pix, embed_weight, level_code, *refs = refs
    else:
        x_own, x_other, *refs = refs
    (
        own_depth, own_gain, own_ub, own_db, oth_depth, oth_gain, oth_ub, oth_db,
        own_up, own_dn, oth_up, oth_dn, out,
        xpad, taps, normed, acc, upb, dnb, sems, *scratch,
    ) = refs
    segment = lax.axis_index("segment")
    place = lax.axis_index("lat")
    width = out.shape[-1]
    hid = own_up.shape[-1]
    blocks = upb.shape[0]
    half = blocks // 2
    low = out.shape[1] // GROUP
    core = lax.rem(segment, 2)
    level = lax.rem(place, out.shape[0] // 2)
    tile = 256
    chunks = width // 128


    def put(r, s, v):
        group = lax.broadcasted_iota(jnp.int32, (GROUP, 128), 0)
        for n in range(chunks):
            part = v[:, 128 * n : 128 * (n + 1)]
            xpad[n, r + 2, s + 2] = part
            for d in (-2, -1, low, low + 1):
                if d % low == s:
                    by = -(d // low)
                    edge = 0 if by > 0 else GROUP - 1
                    moved = pltpu.roll(part, by % GROUP, 0)
                    xpad[n, r + 2, d + 2] = jnp.where(group == edge, 0.0, moved)

    def held(r, s):
        return jnp.concatenate([xpad[n, r + 2, s + 2] for n in range(chunks)], axis=1)

    def copies(b, up, dn):
        return (
            pltpu.make_async_copy(up.at[b % half], upb.at[b], sems.at[0, b]),
            pltpu.make_async_copy(dn.at[b % half], dnb.at[b], sems.at[1, b]),
        )

    @pl.when(segment // 2 == (0 if near else 1))
    def _():
        for b in range(blocks):
            mine = core == b // half

            @pl.when(mine)
            def _():
                for copy in copies(b, own_up, own_dn):
                    copy.start()

            @pl.when(jnp.logical_not(mine))
            def _():
                for copy in copies(b, oth_up, oth_dn):
                    copy.start()

        zero = jnp.zeros((GROUP, 128), xpad.dtype)
        for n in range(chunks):
            for r in range(2):
                for s in range(low + 4):
                    xpad[n, r, s] = zero

        def load_row(r, carry):
            for s in range(low):
                put(r, s, x_own[r, GROUP * s : GROUP * (s + 1), :].astype(jnp.float32))
            return carry

        def load_other(r, carry):
            for s in range(low):
                put(rows - 1 - r, s, x_other[r, GROUP * s : GROUP * (s + 1), :].astype(jnp.float32))
            return carry

        if near:
            cols = GROUP * low
            totals = spread_pixels(pix, embed_weight, level_code, level, *scratch)
            for n in range(rows):
                total = totals[n % len(totals)]
                to = n + core * (rows - 1 - 2 * n)
                for s in range(low):
                    at = (n // len(totals)) * cols + GROUP * s
                    put(to, s, total[at : at + GROUP])
        else:
            lax.fori_loop(0, x_own.shape[0], load_row, 0)
            lax.fori_loop(0, x_other.shape[0], load_other, 0)

        def prepare(b):
            k = b % half
            even, odd = (own_depth, oth_depth) if b < half else (oth_depth, own_depth)
            for i in range(5):
                for j in range(5):
                    p, q = 5 * i + j, 5 * (4 - i) + j
                    tap = jnp.where(
                        core == 1,
                        odd[q, k : k + 1, :].astype(jnp.float32),
                        even[p, k : k + 1, :].astype(jnp.float32),
                    )
                    for n in range(chunks):
                        taps[b % 2, n, p] = jnp.broadcast_to(
                            tap[:, 128 * n : 128 * (n + 1)], (8, 128)
                        )

        def chosen(b, own, oth):
            line = slice(b % half, b % half + 1)
            even, odd = (own, oth) if b < half else (oth, own)
            return jnp.where(
                core == 1, odd[line, :].astype(jnp.float32), even[line, :].astype(jnp.float32)
            )

        prepare(0)
        for b in range(blocks):
            kept = rows - 2 * (b + 1)
            gain = chosen(b, own_gain, oth_gain)
            shift = chosen(b, own_db, oth_db)
            ub = chosen(b, own_ub, oth_ub)

            def conv_rows(n, carry, b=b):
                t = n // chunks
                chunk = n % chunks
                lanes = pl.ds(pl.multiple_of(chunk * 128, 128), 128)
                sums = [[None] * low for _ in range(2)]

                def line(r):
                    return [
                        xpad[chunk, 2 * t + r, s].astype(jnp.bfloat16) for s in range(low + 4)
                    ]

                window = [line(0)]
                for i in range(5):
                    window = [*window[-1:], line(i + 1)]
                    tap = []
                    for j in range(5):
                        w = taps[b % 2, chunk, 5 * i + j]
                        tap.append(jnp.concatenate([w, w], axis=0).astype(jnp.bfloat16))
                    for o in range(2):
                        for s in range(low):
                            part = window[o][s] * tap[0]
                            for j in range(1, 5):
                                part = part + window[o][s + j] * tap[j]
                            sums[o][s] = part if i == 0 else sums[o][s] + part
                for o in range(2):
                    for s in range(low):
                        at = pl.multiple_of(((2 * t + o) * low + s) * GROUP, GROUP)
                        acc[pl.ds(at, GROUP), lanes] = sums[o][s].astype(jnp.float32)
                return carry

            lax.fori_loop(0, kept // 2 * chunks, conv_rows, 0, unroll=UNROLL)
            part = kept * low * GROUP // 2

            def norm_rows(t, gain=gain, part=part):
                at = pl.ds(pl.multiple_of(t * part, part), part)
                v = acc[at, :]
                d = v - jnp.mean(v, axis=-1, keepdims=True)
                spread = jnp.mean(d * d, axis=-1, keepdims=True)
                normed[at, :] = (d * lax.rsqrt(spread + EPSILON) * gain).astype(jnp.bfloat16)

            norm_rows(0)
            for copy in copies(b, own_up, own_dn):
                copy.wait()

            turn = 0 if near else kept - 2 * level
            for t in range(2):
                at = slice(t * part, (t + 1) * part)
                nv = normed[at, :]
                if t == 0:
                    norm_rows(1)
                elif b + 1 < blocks:
                    prepare(b + 1)
                parts = []
                for n in range(hid // tile):
                    cut = slice(n * tile, (n + 1) * tile)
                    h = jnp.dot(nv, upb[b, :, cut], preferred_element_type=jnp.float32)
                    h = h + ub[:, cut]
                    parts.append((0.5 * h * (1.0 + lax.erf(h * (2.0**-0.5)))).astype(jnp.bfloat16))
                branch = jnp.dot(
                    jnp.concatenate(parts, axis=1), dnb[b], preferred_element_type=jnp.float32
                )
                for r in range(kept // 2):
                    row = t * (kept // 2) + r
                    for s in range(low):
                        lines = slice((r * low + s) * GROUP, (r * low + s + 1) * GROUP)
                        v = held(row, s) + branch[lines] + shift
                        if b + 1 < blocks:
                            put(row, s, v)
                        else:
                            to = lax.rem(row + turn, kept)
                            out[to, GROUP * s : GROUP * (s + 1), :] = v.astype(out.dtype)


def placed(x):
    return pltpu.with_memory_space_constraint(x, pltpu.VMEM)


def kept_out(x):
    return pltpu.with_memory_space_constraint(x, pltpu.HBM)


def stage(near, xs, cols, width, smalls, own_up, own_dn, oth_up, oth_dn):
    rows = 2 * xs[0].shape[0]
    blocks = 2 * own_up.shape[0]
    hid = own_up.shape[-1]
    kept = rows - 2 * blocks
    low = cols // GROUP
    vmem = pl.BlockSpec(memory_space=pltpu.VMEM)
    hbm = pl.BlockSpec(memory_space=pltpu.HBM)
    work = (rows * blocks - blocks * (blocks + 1)) * cols
    scratch = [
        pltpu.VMEM((width // 128, rows + 2, low + 4, GROUP, 128), jnp.float32),
        pltpu.VMEM((2, width // 128, 25, 8, 128), jnp.float32),
        pltpu.VMEM((rows * cols, width), jnp.bfloat16),
        pltpu.VMEM((rows * cols, width), jnp.float32),
        pltpu.VMEM((blocks, width, hid), jnp.bfloat16),
        pltpu.VMEM((blocks, hid, width), jnp.bfloat16),
        pltpu.SemaphoreType.DMA((2, blocks)),
    ]
    if near:
        bands, variables, lines, _ = xs[0].shape
        scratch += [
            pltpu.VMEM((PATCH, bands * cols, variables * lines), jnp.bfloat16),
            pltpu.VMEM((variables * lines, width), jnp.bfloat16),
        ]
    return pl.pallas_call(
        functools.partial(stage_kernel, rows, near),
        out_shape=pltpu.VMEM((kept, cols, width), jnp.bfloat16),
        in_specs=[vmem] * (len(xs) + len(smalls)) + [hbm] * 2 + [vmem if near else hbm] * 2,
        out_specs=vmem,
        scratch_shapes=scratch,
        compiler_params=pltpu.CompilerParams(vmem_limit_bytes=VMEM_LIMIT),
        cost_estimate=pl.CostEstimate(
            flops=8 * work * width * hid,
            bytes_accessed=4 * blocks * width * hid,
            transcendentals=work * hid,
        ),
        name="near_stage" if near else "far_stage",
    )(
        placed(xs[0]),
        *((kept_out(x) if near else placed(x)) for x in xs[1:]),
        *(kept_out(x) for x in smalls[:4]),
        *(placed(x) for x in smalls[4:]),
        kept_out(own_up),
        kept_out(own_dn),
        *((placed if near else kept_out)(w) for w in (oth_up, oth_dn)),
    )


def fold_kernel(*refs):
    levels = len(refs) - 8
    xs = refs[:levels]
    gain, latents, memory_weight, output_weight, out, kv, mixed, shown = refs[levels:]
    rows, cols, width = xs[0].shape
    places = rows * cols
    low = cols // GROUP
    scale = HSZ**-0.5
    for i in range(levels):
        v = xs[i][...].reshape(places, width).astype(jnp.float32)
        d = v - jnp.mean(v, axis=-1, keepdims=True)
        spread = jnp.mean(d * d, axis=-1, keepdims=True)
        n = (d * lax.rsqrt(spread + EPSILON) * gain[...].astype(jnp.float32)).astype(jnp.bfloat16)
        kv[i * places : (i + 1) * places, :] = jnp.dot(
            n, memory_weight[...], preferred_element_type=jnp.float32
        ).astype(jnp.bfloat16)
    lat = latents[...].astype(jnp.float32)
    pairs = NLAT * HEADS
    at_row = lax.broadcasted_iota(jnp.int32, (pairs, width), 0)
    at_col = lax.broadcasted_iota(jnp.int32, (pairs, width), 1)
    head = at_col // HSZ == at_row % HEADS
    wide = jnp.concatenate(
        [jnp.broadcast_to(lat[q : q + 1], (HEADS, width)) for q in range(NLAT)], axis=0
    )
    queries = jnp.where(head, wide, 0.0).astype(jnp.bfloat16)
    raised = []
    for i in range(levels):
        s = lax.dot_general(
            kv[i * places : (i + 1) * places, :width],
            queries,
            (((1,), (1,)), ((), ())),
            preferred_element_type=jnp.float32,
        )
        raised.append(jnp.exp(s * scale))
    total = raised[0]
    for i in range(1, levels):
        total = total + raised[i]
    shares = [(r / total).astype(jnp.bfloat16) for r in raised]
    for q in range(NLAT):
        pick = jnp.where(jnp.logical_and(head, at_row // HEADS == q), 1.0, 0.0).astype(jnp.bfloat16)
        m = None
        for i in range(levels):
            w = jnp.dot(shares[i], pick, preferred_element_type=jnp.float32)
            term = w * kv[i * places : (i + 1) * places, width:].astype(jnp.float32)
            m = term if m is None else m + term
        mixed[q * places : (q + 1) * places, :] = m.astype(jnp.bfloat16)
    folded = jnp.dot(mixed[...], output_weight[...], preferred_element_type=jnp.float32)
    flip = (lax.axis_index("lat") >= levels).astype(jnp.int32)
    for q in range(NLAT):
        for r in range(rows):
            for s in range(cols // 8):
                at = q * places + r * cols + 8 * s
                row = r + flip * (rows - 1 - 2 * r)
                group, first = divmod(8 * s, GROUP)
                start = (row * NLAT + q) * cols + first * low + group
                for lane in range(0, width, 128):
                    shown[lane // 128, pl.ds(start, 8, stride=low), :] = (
                        folded[at : at + 8, lane : lane + 128] + lat[q : q + 1, lane : lane + 128]
                    )
    for lane in range(0, width, 128):
        v = shown[lane // 128].astype(out.dtype)
        out[:, :, :, lane : lane + 128] = v.reshape(rows, NLAT, cols, 128)


def fold(xs, gain, latents, memory_weight, output_weight):
    rows, cols, width = xs[0].shape
    places = rows * cols
    vmem = pl.BlockSpec(memory_space=pltpu.VMEM)
    return pl.pallas_call(
        fold_kernel,
        out_shape=jax.ShapeDtypeStruct((rows, NLAT, cols, width), jnp.bfloat16),
        in_specs=[vmem] * (len(xs) + 4),
        out_specs=vmem,
        scratch_shapes=[
            pltpu.VMEM((len(xs) * places, 2 * width), jnp.bfloat16),
            pltpu.VMEM((NLAT * places, width), jnp.bfloat16),
            pltpu.VMEM((width // 128, NLAT * places, 128), jnp.float32),
        ],
        cost_estimate=pl.CostEstimate(
            flops=4 * len(xs) * places * width * width, bytes_accessed=2_000_000, transcendentals=0
        ),
        name="fold",
    )(
        *(placed(x) for x in (*xs, gain, latents, memory_weight, output_weight))
    )


def fits(mesh, shapes):
    pixels, embed_weight, depth, up = shapes[0], shapes[1], shapes[3], shapes[5]
    micro, levels, _, height, wide = pixels
    lat, segment = mesh.shape["lat"], mesh.shape["segment"]
    rows, cols = height // PATCH, wide // PATCH
    blocks = depth[0] // 2 * depth[1]
    return (
        segment == 4
        and depth[0] == segment
        and micro == segment
        and micro * levels == 2 * lat
        and rows == 2 * lat
        and rows == 4 * blocks
        and cols % 32 == 0
        and wide == 128
        and lat == 2 * levels
        and up[2] % 256 == 0
        and embed_weight[1] % 256 == 0
    )


def on_columns(
    pixels,
    embed_weight,
    level_code,
    depth_kernel,
    norm_gain,
    up_weight,
    up_bias,
    down_weight,
    down_bias,
    fold_gain,
    latents,
    memory_weight,
    output_weight,
):
    seg = lax.axis_index("segment")
    lat = lax.axis_size("lat")
    micro, levels, variables, height, wide = pixels.shape
    cols = wide // PATCH
    width = embed_weight.shape[1]
    far = seg // 2

    swap = [(0, 1), (1, 0), (2, 3), (3, 2)]
    own = (depth_kernel[0].transpose(1, 0, 2), norm_gain[0], up_bias[0], down_bias[0])
    own_up, own_dn = up_weight[0], down_weight[0]
    oth = tuple(lax.ppermute(w, "segment", swap) for w in own)
    oth_up = lax.ppermute(own_up, "segment", swap)
    oth_dn = lax.ppermute(own_dn, "segment", swap)
    weights = (own + oth, own_up, own_dn, oth_up, oth_dn)

    got = lax.all_to_all(
        pixels.reshape(2, lat, variables, height, wide), "lat", 1, 1, tiled=True
    )

    onward = [(0, 2), (1, 3)]
    across = [(2, 3), (3, 2)]
    sent = []
    for i in range(2):
        a = stage(True, (got[i], embed_weight, level_code), cols, width, *weights)
        if i:
            a, sent[0] = lax.optimization_barrier((a, sent[0]))
        sent.append(lax.ppermute(a, "segment", onward))
    done = []
    for i in range(2):
        if i:
            done[0], sent[i] = lax.optimization_barrier((done[0], sent[i]))
        other = lax.ppermute(sent[i], "segment", across)
        done.append(stage(False, (sent[i], other), cols, width, *weights))
    home = lax.ppermute(done[0], "segment", [(j, i) for i, j in onward])

    pieces = []
    for t in range(levels):
        pairs = []
        for s in range(4):
            for l in range(lat):
                k = (l % levels + t) % levels
                to_lat = k if s % 2 == 0 else lat - 1 - k
                to_seg = 2 * (s // 2) + l // levels
                pairs.append((s * lat + l, to_seg * lat + to_lat))
        piece = jnp.where(far == 0, home[2 * t : 2 * t + 2], done[1][2 * t : 2 * t + 2])
        pieces.append(lax.ppermute(piece, ("segment", "lat"), pairs))
    folded = fold(pieces, fold_gain[None, :], latents, memory_weight, output_weight)
    return folded.transpose(0, 2, 1, 3)[None]


def solution(mesh):
    specs = (
        P(None, None, None, "lat", None),
        P(),
        P(),
        P("segment", None, None, None),
        P("segment", None, None),
        P("segment", None, None, None),
        P("segment", None, None),
        P("segment", None, None, None),
        P("segment", None, None),
        P(),
        P(),
        P(),
        P(),
    )

    def program(*arrays):
        body = on_columns if fits(mesh, [a.shape for a in arrays]) else on_device
        return jax.shard_map(
            body,
            mesh=mesh,
            in_specs=specs,
            out_specs=P("segment", "lat", None, None, None),
            check_vma=False,
        )(*arrays)

    return program
```

```python
import functools

import jax
import jax.numpy as jnp
from jax import lax
from jax.experimental import pallas as pl
from jax.experimental.pallas import tpu as pltpu
from jax.sharding import PartitionSpec as P

HEADS = 16
HSZ = 32
PATCH = 4
NLAT = 3
BLOCKS = 2


EPSILON = 1e-06


VMEM_LIMIT = 16 * 1024 * 1024
GROUP = 16
UNROLL = 4

def extended(x, sides, width):
    for axis, dim in sides:
        size, length = (lax.axis_size(axis), x.shape[dim])
        up = [(i, (i + 1) % size) for i in range(size - 1)]
        down = [(j, i) for i, j in up]
        last = lax.slice_in_dim(x, length - width, length, axis=dim)
        first = lax.slice_in_dim(x, 0, width, axis=dim)
        before = lax.ppermute(last, axis, up)
        after = lax.ppermute(first, axis, down)
        x = jnp.concatenate([before, x, after], axis=dim)
    return x


def normalize(values_in, gain):
    average = jnp.mean(values_in, axis=-1, keepdims=True)
    centred = values_in - average
    spread_sq = jnp.mean(centred * centred, axis=-1, keepdims=True)
    return centred * lax.rsqrt(spread_sq + EPSILON) * gain.astype(jnp.float32)


def depthwise(padded, kernel, row_count, col_count):
    conv_out = jnp.zeros((padded.shape[0], row_count, col_count, padded.shape[3]), jnp.float32)
    for row_off in range(5):
        for col_off in range(5):
            window = padded[
                :, row_off : row_off + row_count, col_off : col_off + col_count, :
            ].astype(jnp.float32)
            conv_out = conv_out + window * kernel[row_off * 5 + col_off].astype(jnp.float32)
    return conv_out


def conv_block(features, padded_rows, kernel, gain, up_mat, up_shift, down_mat, down_shift):
    padded = jnp.pad(padded_rows, ((0, 0), (0, 0), (2, 2), (0, 0)))
    row_count = features.shape[1]
    col_count = features.shape[2]
    width = features.shape[3]
    conv_out = depthwise(padded, kernel, row_count, col_count)
    normed = normalize(conv_out, gain).astype(jnp.bfloat16)
    flat_rows = normed.reshape(-1, width)
    hidden = jax.nn.gelu(
        jnp.dot(flat_rows, up_mat, preferred_element_type=jnp.float32)
        + up_shift.astype(jnp.float32),
        approximate=False,
    ).astype(jnp.bfloat16)
    branch = jnp.dot(hidden, down_mat, preferred_element_type=jnp.float32) + down_shift.astype(
        jnp.float32
    )
    return (features.astype(jnp.float32) + branch.reshape(features.shape)).astype(jnp.bfloat16)


def embed_patches(sample_pixels, embed_weight, level_code):
    levels = sample_pixels.shape[0]
    variables = sample_pixels.shape[1]
    row_count = sample_pixels.shape[2] // PATCH
    col_count = sample_pixels.shape[3] // PATCH
    patches = sample_pixels.reshape(levels, variables, row_count, PATCH, col_count, PATCH)
    patches = patches.transpose(0, 2, 4, 1, 3, 5).reshape(
        levels * row_count * col_count, variables * PATCH * PATCH
    )
    embedded = jnp.dot(patches, embed_weight, preferred_element_type=jnp.float32).reshape(
        levels, row_count, col_count, -1
    )
    embedded = embedded + level_code[:, None, None, :].astype(jnp.float32)
    return embedded.astype(jnp.bfloat16)


def fold_levels(features, fold_gain, latents, memory_weight, output_weight):
    levels, row_count, col_count, width = features.shape
    places = row_count * col_count
    normed = (
        normalize(features.astype(jnp.float32), fold_gain)
        .astype(jnp.bfloat16)
        .reshape(levels * places, width)
    )
    keyval = jnp.dot(normed, memory_weight, preferred_element_type=jnp.float32).astype(jnp.bfloat16)
    keyval = keyval.reshape(levels, places, 2, HEADS, HSZ)
    queries = latents.reshape(NLAT, HEADS, HSZ)
    scores = jnp.einsum(
        "lphe,qhe->pqlh", keyval[:, :, 0], queries, preferred_element_type=jnp.float32
    ) * HSZ ** (-0.5)
    raised = jnp.exp(scores)
    share = (raised / jnp.sum(raised, axis=2, keepdims=True)).astype(jnp.bfloat16)
    mixed = jnp.einsum(
        "pqlh,lphe->pqhe", share, keyval[:, :, 1], preferred_element_type=jnp.float32
    )
    mixed = mixed.astype(jnp.bfloat16).reshape(places * NLAT, width)
    folded = jnp.dot(mixed, output_weight, preferred_element_type=jnp.float32).reshape(
        places, NLAT, width
    )
    folded = folded + latents.astype(jnp.float32)[None, :, :]
    return folded.astype(jnp.bfloat16).reshape(row_count, col_count, NLAT, width)


def run_section(features, section_weights):
    for block_id in range(BLOCKS):
        padded_rows = extended(features, (("lat", 1),), 2)
        features = conv_block(
            features,
            padded_rows,
            section_weights[0][block_id],
            section_weights[1][block_id],
            section_weights[2][block_id],
            section_weights[3][block_id],
            section_weights[4][block_id],
            section_weights[5][block_id],
        )
    return features


def on_device(
    pixels,
    embed_weight,
    level_code,
    depth_kernel,
    norm_gain,
    up_weight,
    up_bias,
    down_weight,
    down_bias,
    fold_gain,
    latents,
    memory_weight,
    output_weight,
):
    segment_index = lax.axis_index("segment")
    sections = lax.axis_size("segment")
    count_all = pixels.shape[0]
    per_segment = count_all // sections

    def fold_one(features):
        return fold_levels(features, fold_gain, latents, memory_weight, output_weight)

    all_weights = (
        lax.all_gather(depth_kernel, "segment", axis=0, tiled=True),
        lax.all_gather(norm_gain, "segment", axis=0, tiled=True),
        lax.all_gather(up_weight, "segment", axis=0, tiled=True),
        lax.all_gather(up_bias, "segment", axis=0, tiled=True),
        lax.all_gather(down_weight, "segment", axis=0, tiled=True),
        lax.all_gather(down_bias, "segment", axis=0, tiled=True),
    )
    own_pixels = lax.dynamic_slice_in_dim(pixels, segment_index * per_segment, per_segment, 0)

    def per_sample(sample_pixels):
        features = embed_patches(sample_pixels, embed_weight, level_code)
        for section_id in range(sections):
            features = run_section(
                features, tuple((weight_set[section_id] for weight_set in all_weights))
            )
        return fold_one(features)

    return lax.map(per_sample, own_pixels)


def spread_pixels(pix, by_col, code, diagonal, spread):
    bands, variables, lines, wide = pix.shape
    cols = wide // PATCH
    low = cols // GROUP
    taken = variables * lines
    at = lax.broadcasted_iota(jnp.int32, (cols, PATCH * wide), 1)
    spot = lax.broadcasted_iota(jnp.int32, (cols, PATCH * wide), 0)
    source = ((spot % GROUP) * low + spot // GROUP) * PATCH + at // wide
    pick = jnp.where(source == at % wide, 1.0, 0.0).astype(jnp.bfloat16)
    for slot in range(2):
        diagonal[slot] = jnp.zeros(diagonal.shape[1:], diagonal.dtype)
    for n in range(bands):
        slot = n % 2
        for p in range(PATCH):
            diagonal[slot, p * taken : (p + 1) * taken, p * wide : (p + 1) * wide] = pix[n].reshape(
                taken, wide
            )
        spread[n * cols : (n + 1) * cols, :] = lax.dot_general(
            pick, diagonal[slot], (((1,), (1,)), ((), ())), preferred_element_type=jnp.float32
        ).astype(jnp.bfloat16)
    return [
        jnp.dot(spread[...], by_col[b], preferred_element_type=jnp.float32) + code
        for b in range(by_col.shape[0])
    ]


def lay_out(core, level, lines, own, oth, weight, code, taps, vecs, by_col):
    depth, gain, ub, db = range(4)
    half, width = own[db].shape
    for b in range(2 * half):
        line = slice(b % half, b % half + 1)

        def chosen(n, even, odd, b=b):
            a, c = (own[n], oth[n]) if b < half else (oth[n], own[n])
            return jnp.where(core == 1, c[odd].astype(jnp.float32), a[even].astype(jnp.float32))

        for i in range(5):
            for j in range(5):
                p, q = 5 * i + j, 5 * (4 - i) + j
                tap = chosen(depth, (p, line), (q, line))
                for n in range(width // 128):
                    taps[b, n, p] = jnp.broadcast_to(tap[:, 128 * n : 128 * (n + 1)], (8, 128))
        at = (line, slice(None))
        vecs[b, 0:1, :] = chosen(ub, at, at)
        vecs[b, 1:2, 0:width] = chosen(gain, at, at)
        vecs[b, 2:3, 0:width] = chosen(db, at, at)
    shown = code[0:1, :].astype(jnp.float32)
    for n in range(1, code.shape[0]):
        shown = jnp.where(level == n, code[n : n + 1, :].astype(jnp.float32), shown)
    vecs[0, 3:4, 0:width] = shown
    deep = weight.shape[0]
    taken = deep // (PATCH * PATCH) * lines
    row = lax.broadcasted_iota(jnp.int32, (PATCH * taken, deep), 0)
    source = lax.broadcasted_iota(jnp.int32, (PATCH * taken, deep), 1)
    to = row % taken
    base = (to // lines) * (PATCH * PATCH) + (to % PATCH) * PATCH + row // taken
    for b in range(lines // PATCH):
        same = jnp.logical_and(base == source, (to % lines) // PATCH == b)
        by_col[b] = jnp.dot(
            jnp.where(same, 1.0, 0.0).astype(jnp.bfloat16),
            weight[...],
            preferred_element_type=jnp.float32,
        ).astype(jnp.bfloat16)


def stage_kernel(rows, kind, *refs):
    first, near = kind == "first", kind != "far"
    if first:
        pix, *stored = refs[:15]
        out, up, dn, taps, vecs, by_col, xpad, normed, acc, diagonal, spread, *held_small, sems = refs[15:]
    elif near:
        pix, by_col, up, dn, taps, vecs, out, xpad, normed, acc, diagonal, spread = refs
    else:
        x_own, x_other, up, dn, taps, vecs, out, xpad, normed, acc = refs
    segment = lax.axis_index("segment")
    place = lax.axis_index("lat")
    width = out.shape[-1]
    blocks, _, hid = up.shape
    low = out.shape[1] // GROUP
    core = lax.rem(segment, 2)
    level = lax.rem(place, out.shape[0] // 2)
    tile = 256
    chunks = width // 128


    def put(r, s, v):
        group = lax.broadcasted_iota(jnp.int32, (GROUP, 128), 0)
        for n in range(chunks):
            part = v[:, 128 * n : 128 * (n + 1)]
            xpad[n, r + 2, s + 2] = part
            for d in (-2, -1, low, low + 1):
                if d % low == s:
                    by = -(d // low)
                    edge = 0 if by > 0 else GROUP - 1
                    moved = pltpu.roll(part, by % GROUP, 0)
                    xpad[n, r + 2, d + 2] = jnp.where(group == edge, 0.0, moved)

    def held(r, s):
        return jnp.concatenate([xpad[n, r + 2, s + 2] for n in range(chunks)], axis=1)

    active = segment // 2 == (0 if near else 1)
    if first:
        half = blocks // 2
        own, oth = stored[:6], stored[6:12]
        small = [*own[:4], *oth[:4], *stored[12:]]
        arrivals = [
            pltpu.make_async_copy(a, b, sems.at[2, n]) for n, (a, b) in enumerate(zip(small, held_small))
        ]
        for copy in arrivals:
            copy.start()
        for k in range(half):
            for source, start in ((own, core * half), (oth, (1 - core) * half)):
                pltpu.make_async_copy(source[4].at[k], up.at[start + k], sems.at[0, start + k]).start()
                pltpu.make_async_copy(source[5].at[k], dn.at[start + k], sems.at[1, start + k]).start()
        for copy in arrivals:
            copy.wait()
        lay_out(
            core, level, pix.shape[2], held_small[:4], held_small[4:8], *held_small[8:], taps, vecs, by_col
        )

    def weights_in(b):
        if first:
            k = b % (blocks // 2)
            pltpu.make_async_copy(stored[4].at[k], up.at[b], sems.at[0, b]).wait()
            pltpu.make_async_copy(stored[5].at[k], dn.at[b], sems.at[1, b]).wait()

    @pl.when(jnp.logical_not(active))
    def _():
        for b in range(blocks):
            weights_in(b)

    @pl.when(active)
    def _():
        zero = jnp.zeros((GROUP, 128), xpad.dtype)
        for n in range(chunks):
            for r in range(2):
                for s in range(low + 4):
                    xpad[n, r, s] = zero

        def load_row(r, carry):
            for s in range(low):
                put(r, s, x_own[r, GROUP * s : GROUP * (s + 1), :].astype(jnp.float32))
            return carry

        def load_other(r, carry):
            for s in range(low):
                put(rows - 1 - r, s, x_other[r, GROUP * s : GROUP * (s + 1), :].astype(jnp.float32))
            return carry

        if near:
            cols = GROUP * low
            totals = spread_pixels(pix, by_col, vecs[0, 3:4, 0:width], diagonal, spread)
            for n in range(rows):
                total = totals[n % len(totals)]
                to = n + core * (rows - 1 - 2 * n)
                for s in range(low):
                    at = (n // len(totals)) * cols + GROUP * s
                    put(to, s, total[at : at + GROUP])
        else:
            lax.fori_loop(0, x_own.shape[0], load_row, 0)
            lax.fori_loop(0, x_other.shape[0], load_other, 0)

        for b in range(blocks):
            kept = rows - 2 * (b + 1)
            ub = vecs[b, 0:1, :]
            gain = vecs[b, 1:2, 0:width]
            shift = vecs[b, 2:3, 0:width]

            def conv_rows(n, carry, b=b):
                t = n // chunks
                chunk = n % chunks
                lanes = pl.ds(pl.multiple_of(chunk * 128, 128), 128)
                sums = [[None] * low for _ in range(2)]

                def line(r):
                    return [
                        xpad[chunk, 2 * t + r, s].astype(jnp.bfloat16) for s in range(low + 4)
                    ]

                window = [line(0)]
                for i in range(5):
                    window = [*window[-1:], line(i + 1)]
                    tap = []
                    for j in range(5):
                        w = taps[b, chunk, 5 * i + j]
                        tap.append(jnp.concatenate([w, w], axis=0).astype(jnp.bfloat16))
                    for o in range(2):
                        for s in range(low):
                            part = window[o][s] * tap[0]
                            for j in range(1, 5):
                                part = part + window[o][s + j] * tap[j]
                            sums[o][s] = part if i == 0 else sums[o][s] + part
                for o in range(2):
                    for s in range(low):
                        at = pl.multiple_of(((2 * t + o) * low + s) * GROUP, GROUP)
                        acc[pl.ds(at, GROUP), lanes] = sums[o][s].astype(jnp.float32)
                return carry

            lax.fori_loop(0, kept // 2 * chunks, conv_rows, 0, unroll=UNROLL)
            part = kept * low * GROUP // 2

            def norm_rows(t, gain=gain, part=part):
                at = pl.ds(pl.multiple_of(t * part, part), part)
                v = acc[at, :]
                d = v - jnp.mean(v, axis=-1, keepdims=True)
                spread = jnp.mean(d * d, axis=-1, keepdims=True)
                normed[at, :] = (d * lax.rsqrt(spread + EPSILON) * gain).astype(jnp.bfloat16)

            norm_rows(0)
            weights_in(b)

            turn = 0 if near else kept - 2 * level
            for t in range(2):
                at = slice(t * part, (t + 1) * part)
                nv = normed[at, :]
                if t == 0:
                    norm_rows(1)
                parts = []
                for n in range(hid // tile):
                    cut = slice(n * tile, (n + 1) * tile)
                    h = jnp.dot(nv, up[b, :, cut], preferred_element_type=jnp.float32)
                    h = h + ub[:, cut]
                    parts.append((0.5 * h * (1.0 + lax.erf(h * (2.0**-0.5)))).astype(jnp.bfloat16))
                branch = jnp.dot(
                    jnp.concatenate(parts, axis=1), dn[b], preferred_element_type=jnp.float32
                )
                for r in range(kept // 2):
                    row = t * (kept // 2) + r
                    for s in range(low):
                        lines = slice((r * low + s) * GROUP, (r * low + s + 1) * GROUP)
                        v = held(row, s) + branch[lines] + shift
                        if b + 1 < blocks:
                            put(row, s, v)
                        else:
                            to = lax.rem(row + turn, kept)
                            out[to, GROUP * s : GROUP * (s + 1), :] = v.astype(out.dtype)


def placed(x):
    return pltpu.with_memory_space_constraint(x, pltpu.VMEM)


def kept_out(x):
    return pltpu.with_memory_space_constraint(x, pltpu.HBM)


def stage(kind, xs, cols, weights):
    first, near = kind == "first", kind != "far"
    rows = 2 * xs[0].shape[0]
    if first:
        half, width, hid = weights[4].shape
        blocks = 2 * half
    else:
        blocks, width, hid = weights[0].shape
    kept = rows - 2 * blocks
    low = cols // GROUP
    vmem = pl.BlockSpec(memory_space=pltpu.VMEM)
    hbm = pl.BlockSpec(memory_space=pltpu.HBM)
    work = (rows * blocks - blocks * (blocks + 1)) * cols
    outs = [pltpu.VMEM((kept, cols, width), jnp.bfloat16)]
    scratch = [
        pltpu.VMEM((width // 128, rows + 2, low + 4, GROUP, 128), jnp.float32),
        pltpu.VMEM((rows * cols, width), jnp.bfloat16),
        pltpu.VMEM((rows * cols, width), jnp.float32),
    ]
    if near:
        bands, variables, lines, wide = xs[0].shape
        depth = PATCH * variables * lines
        scratch += [
            pltpu.VMEM((2, depth, PATCH * wide), jnp.bfloat16),
            pltpu.VMEM((bands * cols, depth), jnp.bfloat16),
        ]
    if first:
        outs += [
            pltpu.VMEM((blocks, width, hid), jnp.bfloat16),
            pltpu.VMEM((blocks, hid, width), jnp.bfloat16),
            pltpu.VMEM((blocks, width // 128, 25, 8, 128), jnp.float32),
            pltpu.VMEM((blocks, 8, hid), jnp.float32),
            pltpu.VMEM((lines // PATCH, depth, width), jnp.bfloat16),
        ]
        small = [*weights[:4], *weights[6:10], *weights[12:]]
        scratch += [pltpu.VMEM(w.shape, w.dtype) for w in small]
        scratch += [pltpu.SemaphoreType.DMA((3, max(blocks, len(small))))]
    stays = [first and n != 10 for n in range(len(weights))]
    operands = [placed(x) for x in xs]
    operands += [kept_out(w) if stay else placed(w) for w, stay in zip(weights, stays)]
    return pl.pallas_call(
        functools.partial(stage_kernel, rows, kind),
        out_shape=tuple(outs),
        in_specs=[vmem] * len(xs) + [hbm if stay else vmem for stay in stays],
        out_specs=(vmem,) * len(outs),
        scratch_shapes=scratch,
        compiler_params=pltpu.CompilerParams(vmem_limit_bytes=VMEM_LIMIT),
        cost_estimate=pl.CostEstimate(
            flops=8 * work * width * hid,
            bytes_accessed=4 * blocks * width * hid,
            transcendentals=work * hid,
        ),
        name=kind + "_stage",
    )(*operands)


def choose_kernel(home, last, *pieces):
    rows = pieces[0].shape[0]
    near = lax.axis_index("segment") // 2 == 0
    for flag, source in ((near, home), (jnp.logical_not(near), last)):

        @pl.when(flag)
        def _():
            for t, piece in enumerate(pieces):
                piece[...] = source[t * rows : (t + 1) * rows]


def choose(home, last, count):
    vmem = pl.BlockSpec(memory_space=pltpu.VMEM)
    rows, cols, width = last.shape
    return pl.pallas_call(
        choose_kernel,
        out_shape=(pltpu.VMEM((rows // count, cols, width), last.dtype),) * count,
        in_specs=[vmem] * 2,
        out_specs=(vmem,) * count,
        compiler_params=pltpu.CompilerParams(vmem_limit_bytes=VMEM_LIMIT),
        cost_estimate=pl.CostEstimate(flops=0, bytes_accessed=4 * last.size, transcendentals=0),
        name="choose",
    )(placed(home), placed(last))


def fold_kernel(*refs):
    levels = len(refs) - 8
    xs = refs[:levels]
    gain, latents, memory_weight, output_weight, out, kv, mixed, shown = refs[levels:]
    rows, cols, width = xs[0].shape
    places = rows * cols
    low = cols // GROUP
    scale = HSZ**-0.5
    for i in range(levels):
        v = xs[i][...].reshape(places, width).astype(jnp.float32)
        d = v - jnp.mean(v, axis=-1, keepdims=True)
        spread = jnp.mean(d * d, axis=-1, keepdims=True)
        n = (d * lax.rsqrt(spread + EPSILON) * gain[...].astype(jnp.float32)).astype(jnp.bfloat16)
        kv[i * places : (i + 1) * places, :] = jnp.dot(
            n, memory_weight[...], preferred_element_type=jnp.float32
        ).astype(jnp.bfloat16)
    lat = latents[...].astype(jnp.float32)
    pairs = NLAT * HEADS
    at_row = lax.broadcasted_iota(jnp.int32, (pairs, width), 0)
    at_col = lax.broadcasted_iota(jnp.int32, (pairs, width), 1)
    head = at_col // HSZ == at_row % HEADS
    wide = jnp.concatenate(
        [jnp.broadcast_to(lat[q : q + 1], (HEADS, width)) for q in range(NLAT)], axis=0
    )
    queries = jnp.where(head, wide, 0.0).astype(jnp.bfloat16)
    raised = []
    for i in range(levels):
        s = lax.dot_general(
            kv[i * places : (i + 1) * places, :width],
            queries,
            (((1,), (1,)), ((), ())),
            preferred_element_type=jnp.float32,
        )
        raised.append(jnp.exp(s * scale))
    total = raised[0]
    for i in range(1, levels):
        total = total + raised[i]
    shares = [(r / total).astype(jnp.bfloat16) for r in raised]
    for q in range(NLAT):
        pick = jnp.where(jnp.logical_and(head, at_row // HEADS == q), 1.0, 0.0).astype(jnp.bfloat16)
        m = None
        for i in range(levels):
            w = jnp.dot(shares[i], pick, preferred_element_type=jnp.float32)
            term = w * kv[i * places : (i + 1) * places, width:].astype(jnp.float32)
            m = term if m is None else m + term
        mixed[q * places : (q + 1) * places, :] = m.astype(jnp.bfloat16)
    folded = jnp.dot(mixed[...], output_weight[...], preferred_element_type=jnp.float32)
    flip = (lax.axis_index("lat") >= levels).astype(jnp.int32)
    for q in range(NLAT):
        for r in range(rows):
            for s in range(cols // 8):
                at = q * places + r * cols + 8 * s
                row = r + flip * (rows - 1 - 2 * r)
                group, first = divmod(8 * s, GROUP)
                start = (row * NLAT + q) * cols + first * low + group
                for lane in range(0, width, 128):
                    shown[lane // 128, pl.ds(start, 8, stride=low), :] = (
                        folded[at : at + 8, lane : lane + 128] + lat[q : q + 1, lane : lane + 128]
                    )
    for lane in range(0, width, 128):
        v = shown[lane // 128].astype(out.dtype)
        out[:, :, :, lane : lane + 128] = v.reshape(rows, NLAT, cols, 128)


def fold(xs, gain, latents, memory_weight, output_weight):
    rows, cols, width = xs[0].shape
    places = rows * cols
    vmem = pl.BlockSpec(memory_space=pltpu.VMEM)
    return pl.pallas_call(
        fold_kernel,
        out_shape=jax.ShapeDtypeStruct((rows, NLAT, cols, width), jnp.bfloat16),
        in_specs=[vmem] * (len(xs) + 4),
        out_specs=vmem,
        scratch_shapes=[
            pltpu.VMEM((len(xs) * places, 2 * width), jnp.bfloat16),
            pltpu.VMEM((NLAT * places, width), jnp.bfloat16),
            pltpu.VMEM((width // 128, NLAT * places, 128), jnp.float32),
        ],
        cost_estimate=pl.CostEstimate(
            flops=4 * len(xs) * places * width * width,
            bytes_accessed=2_000_000,
            transcendentals=0,
        ),
        compiler_params=pltpu.CompilerParams(vmem_limit_bytes=VMEM_LIMIT),
        name="fold",
    )(
        *(placed(x) for x in (*xs, gain, latents, memory_weight, output_weight))
    )


def fits(mesh, shapes):
    pixels, embed_weight, depth, up = shapes[0], shapes[1], shapes[3], shapes[5]
    micro, levels, _, height, wide = pixels
    lat, segment = mesh.shape["lat"], mesh.shape["segment"]
    rows, cols = height // PATCH, wide // PATCH
    blocks = depth[0] // 2 * depth[1]
    return (
        segment == 4
        and depth[0] == segment
        and micro == segment
        and micro * levels == 2 * lat
        and rows == 2 * lat
        and rows == 4 * blocks
        and cols % 32 == 0
        and wide == 128
        and lat == 2 * levels
        and up[2] % 256 == 0
        and embed_weight[1] % 256 == 0
    )


def on_columns(
    pixels,
    embed_weight,
    level_code,
    depth_kernel,
    norm_gain,
    up_weight,
    up_bias,
    down_weight,
    down_bias,
    fold_gain,
    latents,
    memory_weight,
    output_weight,
):
    lat = lax.axis_size("lat")
    micro, levels, variables, height, wide = pixels.shape
    cols = wide // PATCH
    width = embed_weight.shape[1]

    swap = [(0, 1), (1, 0), (2, 3), (3, 2)]
    own = (depth_kernel[0].transpose(1, 0, 2), norm_gain[0], up_bias[0], down_bias[0])
    own = (*own, up_weight[0], down_weight[0])
    oth = tuple(lax.ppermute(w, "segment", swap) for w in own)
    got = lax.all_to_all(
        pixels.reshape(2, lat, variables, height, wide), "lat", 1, 1, tiled=True
    )

    got, oth = lax.optimization_barrier((got, oth))

    onward = [(0, 2), (1, 3)]
    across = [(2, 3), (3, 2)]
    sent = []
    for i in range(2):
        if i == 0:
            a, *weights, by_col = stage("first", (got[i],), cols, (*own, *oth, embed_weight, level_code))
        else:
            (a,) = stage("near", (got[i], by_col), cols, weights)
            a, sent[0] = lax.optimization_barrier((a, sent[0]))
        sent.append(lax.ppermute(a, "segment", onward))
    done = []
    for i in range(2):
        if i:
            done[0], sent[i] = lax.optimization_barrier((done[0], sent[i]))
        other = lax.ppermute(sent[i], "segment", across)
        (a,) = stage("far", (sent[i], other), cols, weights)
        done.append(a)
    home = lax.ppermute(done[0], "segment", [(j, i) for i, j in onward])

    pieces = []
    leaving = choose(home, done[1], levels)
    for t in range(levels):
        pairs = []
        for s in range(4):
            for l in range(lat):
                k = (l % levels + t) % levels
                to_lat = k if s % 2 == 0 else lat - 1 - k
                to_seg = 2 * (s // 2) + l // levels
                pairs.append((s * lat + l, to_seg * lat + to_lat))
        pieces.append(lax.ppermute(leaving[t], ("segment", "lat"), pairs))
    folded = fold(pieces, fold_gain[None, :], latents, memory_weight, output_weight)
    return folded.transpose(0, 2, 1, 3)[None]


def solution(mesh):
    specs = (
        P(None, None, None, "lat", None),
        P(),
        P(),
        P("segment", None, None, None),
        P("segment", None, None),
        P("segment", None, None, None),
        P("segment", None, None),
        P("segment", None, None, None),
        P("segment", None, None),
        P(),
        P(),
        P(),
        P(),
    )

    def program(*arrays):
        body = on_columns if fits(mesh, [a.shape for a in arrays]) else on_device

        return jax.shard_map(
            body,
            mesh=mesh,
            in_specs=specs,
            out_specs=P("segment", "lat", None, None, None),
            check_vma=False,
        )(*arrays)

    return program
```

```python
import functools

import jax
import jax.numpy as jnp
from jax import lax
from jax.experimental import pallas as pl
from jax.experimental.pallas import tpu as pltpu
from jax.sharding import PartitionSpec as P

HEADS = 16
HSZ = 32
PATCH = 4
NLAT = 3
BLOCKS = 2


EPSILON = 1e-06


VMEM_LIMIT = 16 * 1024 * 1024
GROUP = 16
UNROLL = 4

def extended(x, sides, width):
    for axis, dim in sides:
        size, length = (lax.axis_size(axis), x.shape[dim])
        up = [(i, (i + 1) % size) for i in range(size - 1)]
        down = [(j, i) for i, j in up]
        last = lax.slice_in_dim(x, length - width, length, axis=dim)
        first = lax.slice_in_dim(x, 0, width, axis=dim)
        before = lax.ppermute(last, axis, up)
        after = lax.ppermute(first, axis, down)
        x = jnp.concatenate([before, x, after], axis=dim)
    return x


def normalize(values_in, gain):
    average = jnp.mean(values_in, axis=-1, keepdims=True)
    centred = values_in - average
    spread_sq = jnp.mean(centred * centred, axis=-1, keepdims=True)
    return centred * lax.rsqrt(spread_sq + EPSILON) * gain.astype(jnp.float32)


def depthwise(padded, kernel, row_count, col_count):
    conv_out = jnp.zeros((padded.shape[0], row_count, col_count, padded.shape[3]), jnp.float32)
    for row_off in range(5):
        for col_off in range(5):
            window = padded[
                :, row_off : row_off + row_count, col_off : col_off + col_count, :
            ].astype(jnp.float32)
            conv_out = conv_out + window * kernel[row_off * 5 + col_off].astype(jnp.float32)
    return conv_out


def conv_block(features, padded_rows, kernel, gain, up_mat, up_shift, down_mat, down_shift):
    padded = jnp.pad(padded_rows, ((0, 0), (0, 0), (2, 2), (0, 0)))
    row_count = features.shape[1]
    col_count = features.shape[2]
    width = features.shape[3]
    conv_out = depthwise(padded, kernel, row_count, col_count)
    normed = normalize(conv_out, gain).astype(jnp.bfloat16)
    flat_rows = normed.reshape(-1, width)
    hidden = jax.nn.gelu(
        jnp.dot(flat_rows, up_mat, preferred_element_type=jnp.float32)
        + up_shift.astype(jnp.float32),
        approximate=False,
    ).astype(jnp.bfloat16)
    branch = jnp.dot(hidden, down_mat, preferred_element_type=jnp.float32) + down_shift.astype(
        jnp.float32
    )
    return (features.astype(jnp.float32) + branch.reshape(features.shape)).astype(jnp.bfloat16)


def embed_patches(sample_pixels, embed_weight, level_code):
    levels = sample_pixels.shape[0]
    variables = sample_pixels.shape[1]
    row_count = sample_pixels.shape[2] // PATCH
    col_count = sample_pixels.shape[3] // PATCH
    patches = sample_pixels.reshape(levels, variables, row_count, PATCH, col_count, PATCH)
    patches = patches.transpose(0, 2, 4, 1, 3, 5).reshape(
        levels * row_count * col_count, variables * PATCH * PATCH
    )
    embedded = jnp.dot(patches, embed_weight, preferred_element_type=jnp.float32).reshape(
        levels, row_count, col_count, -1
    )
    embedded = embedded + level_code[:, None, None, :].astype(jnp.float32)
    return embedded.astype(jnp.bfloat16)


def fold_levels(features, fold_gain, latents, memory_weight, output_weight):
    levels, row_count, col_count, width = features.shape
    places = row_count * col_count
    normed = (
        normalize(features.astype(jnp.float32), fold_gain)
        .astype(jnp.bfloat16)
        .reshape(levels * places, width)
    )
    keyval = jnp.dot(normed, memory_weight, preferred_element_type=jnp.float32).astype(jnp.bfloat16)
    keyval = keyval.reshape(levels, places, 2, HEADS, HSZ)
    queries = latents.reshape(NLAT, HEADS, HSZ)
    scores = jnp.einsum(
        "lphe,qhe->pqlh", keyval[:, :, 0], queries, preferred_element_type=jnp.float32
    ) * HSZ ** (-0.5)
    raised = jnp.exp(scores)
    share = (raised / jnp.sum(raised, axis=2, keepdims=True)).astype(jnp.bfloat16)
    mixed = jnp.einsum(
        "pqlh,lphe->pqhe", share, keyval[:, :, 1], preferred_element_type=jnp.float32
    )
    mixed = mixed.astype(jnp.bfloat16).reshape(places * NLAT, width)
    folded = jnp.dot(mixed, output_weight, preferred_element_type=jnp.float32).reshape(
        places, NLAT, width
    )
    folded = folded + latents.astype(jnp.float32)[None, :, :]
    return folded.astype(jnp.bfloat16).reshape(row_count, col_count, NLAT, width)


def run_section(features, section_weights):
    for block_id in range(BLOCKS):
        padded_rows = extended(features, (("lat", 1),), 2)
        features = conv_block(
            features,
            padded_rows,
            section_weights[0][block_id],
            section_weights[1][block_id],
            section_weights[2][block_id],
            section_weights[3][block_id],
            section_weights[4][block_id],
            section_weights[5][block_id],
        )
    return features


def on_device(
    pixels,
    embed_weight,
    level_code,
    depth_kernel,
    norm_gain,
    up_weight,
    up_bias,
    down_weight,
    down_bias,
    fold_gain,
    latents,
    memory_weight,
    output_weight,
):
    segment_index = lax.axis_index("segment")
    sections = lax.axis_size("segment")
    count_all = pixels.shape[0]
    per_segment = count_all // sections

    def fold_one(features):
        return fold_levels(features, fold_gain, latents, memory_weight, output_weight)

    all_weights = (
        lax.all_gather(depth_kernel, "segment", axis=0, tiled=True),
        lax.all_gather(norm_gain, "segment", axis=0, tiled=True),
        lax.all_gather(up_weight, "segment", axis=0, tiled=True),
        lax.all_gather(up_bias, "segment", axis=0, tiled=True),
        lax.all_gather(down_weight, "segment", axis=0, tiled=True),
        lax.all_gather(down_bias, "segment", axis=0, tiled=True),
    )
    own_pixels = lax.dynamic_slice_in_dim(pixels, segment_index * per_segment, per_segment, 0)

    def per_sample(sample_pixels):
        features = embed_patches(sample_pixels, embed_weight, level_code)
        for section_id in range(sections):
            features = run_section(
                features, tuple((weight_set[section_id] for weight_set in all_weights))
            )
        return fold_one(features)

    return lax.map(per_sample, own_pixels)


def spread_pixels(pix, by_col, vecs, diagonal, spread, ready):
    bands, variables, lines, wide = pix.shape
    cols = wide // PATCH
    low = cols // GROUP
    taken = variables * lines
    at = lax.broadcasted_iota(jnp.int32, (cols, PATCH * wide), 1)
    spot = lax.broadcasted_iota(jnp.int32, (cols, PATCH * wide), 0)
    source = ((spot % GROUP) * low + spot // GROUP) * PATCH + at // wide
    pick = jnp.where(source == at % wide, 1.0, 0.0).astype(jnp.bfloat16)
    for slot in range(2):
        diagonal[slot] = jnp.zeros(diagonal.shape[1:], diagonal.dtype)
    for n in range(bands):
        slot = n % 2
        for p in range(PATCH):
            diagonal[slot, p * taken : (p + 1) * taken, p * wide : (p + 1) * wide] = pix[n].reshape(
                taken, wide
            )
        spread[n * cols : (n + 1) * cols, :] = lax.dot_general(
            pick, diagonal[slot], (((1,), (1,)), ((), ())), preferred_element_type=jnp.float32
        ).astype(jnp.bfloat16)
    ready()
    code = vecs[0, 3:4, 0 : by_col.shape[-1]]
    return [
        jnp.dot(spread[...], by_col[b], preferred_element_type=jnp.float32) + code
        for b in range(by_col.shape[0])
    ]


def lay_block(b, core, own, oth, taps, vecs):
    depth, gain, ub, db = range(4)
    half, width = own[db].shape
    line = slice(b % half, b % half + 1)

    def chosen(n, even, odd, b=b):
        a, c = (own[n], oth[n]) if b < half else (oth[n], own[n])
        return jnp.where(core == 1, c[odd].astype(jnp.float32), a[even].astype(jnp.float32))

    for i in range(5):
        for j in range(5):
            p, q = 5 * i + j, 5 * (4 - i) + j
            tap = chosen(depth, (p, line), (q, line))
            for n in range(width // 128):
                taps[b, n, p] = jnp.broadcast_to(tap[:, 128 * n : 128 * (n + 1)], (8, 128))
    at = (line, slice(None))
    vecs[b, 0:1, :] = chosen(ub, at, at)
    vecs[b, 1:2, 0:width] = chosen(gain, at, at)
    vecs[b, 2:3, 0:width] = chosen(db, at, at)


def lay_shared(level, lines, weight, code, vecs, by_col):
    width = weight.shape[1]
    shown = code[0:1, :].astype(jnp.float32)
    for n in range(1, code.shape[0]):
        shown = jnp.where(level == n, code[n : n + 1, :].astype(jnp.float32), shown)
    vecs[0, 3:4, 0:width] = shown
    deep = weight.shape[0]
    taken = deep // (PATCH * PATCH) * lines
    row = lax.broadcasted_iota(jnp.int32, (PATCH * taken, deep), 0)
    source = lax.broadcasted_iota(jnp.int32, (PATCH * taken, deep), 1)
    to = row % taken
    base = (to // lines) * (PATCH * PATCH) + (to % PATCH) * PATCH + row // taken
    for b in range(lines // PATCH):
        same = jnp.logical_and(base == source, (to % lines) // PATCH == b)
        by_col[b] = jnp.dot(
            jnp.where(same, 1.0, 0.0).astype(jnp.bfloat16),
            weight[...],
            preferred_element_type=jnp.float32,
        ).astype(jnp.bfloat16)


def stage_kernel(rows, kind, *refs):
    first, near = kind == "first", kind != "far"
    if first:
        pix, *stored = refs[:15]
        out, up, dn, taps, vecs, by_col, xpad, normed, acc, diagonal, spread, *held_small, sems = refs[15:]
    elif near:
        pix, by_col, up, dn, taps, vecs, out, xpad, normed, acc, diagonal, spread = refs
    else:
        x_own, x_other, up, dn, taps, vecs, out, xpad, normed, acc = refs
    segment = lax.axis_index("segment")
    place = lax.axis_index("lat")
    width = out.shape[-1]
    blocks, _, hid = up.shape
    low = out.shape[1] // GROUP
    core = lax.rem(segment, 2)
    level = lax.rem(place, out.shape[0] // 2)
    tile = 256
    chunks = width // 128


    def put(r, s, v):
        group = lax.broadcasted_iota(jnp.int32, (GROUP, 128), 0)
        for n in range(chunks):
            part = v[:, 128 * n : 128 * (n + 1)]
            xpad[n, r + 2, s + 2] = part
            for d in (-2, -1, low, low + 1):
                if d % low == s:
                    by = -(d // low)
                    edge = 0 if by > 0 else GROUP - 1
                    moved = pltpu.roll(part, by % GROUP, 0)
                    xpad[n, r + 2, d + 2] = jnp.where(group == edge, 0.0, moved)

    def held(r, s):
        return jnp.concatenate([xpad[n, r + 2, s + 2] for n in range(chunks)], axis=1)

    active = segment // 2 == (0 if near else 1)
    if first:
        half = blocks // 2
        own, oth = stored[:6], stored[6:12]
        small = [*own[:4], *oth[:4], *stored[12:]]
        arrivals = [
            pltpu.make_async_copy(a, b, sems.at[2, n]) for n, (a, b) in enumerate(zip(small, held_small))
        ]
        for copy in arrivals:
            copy.start()
        for k in range(half):
            for source, start in ((own, core * half), (oth, (1 - core) * half)):
                pltpu.make_async_copy(source[4].at[k], up.at[start + k], sems.at[0, start + k]).start()
                pltpu.make_async_copy(source[5].at[k], dn.at[start + k], sems.at[1, start + k]).start()

    def lay(b):
        if first and b < blocks:
            lay_block(b, core, held_small[:4], held_small[4:8], taps, vecs)

    def ready():
        if first:
            for copy in arrivals:
                copy.wait()
            lay_shared(level, pix.shape[2], *held_small[8:], vecs, by_col)
            lay(0)

    def weights_in(b):
        if first:
            k = b % (blocks // 2)
            pltpu.make_async_copy(stored[4].at[k], up.at[b], sems.at[0, b]).wait()
            pltpu.make_async_copy(stored[5].at[k], dn.at[b], sems.at[1, b]).wait()

    @pl.when(jnp.logical_not(active))
    def _():
        ready()
        for b in range(blocks):
            if b:
                lay(b)
            weights_in(b)

    @pl.when(active)
    def _():
        zero = jnp.zeros((GROUP, 128), xpad.dtype)
        for n in range(chunks):
            for r in range(2):
                for s in range(low + 4):
                    xpad[n, r, s] = zero

        def load_row(r, carry):
            for s in range(low):
                put(r, s, x_own[r, GROUP * s : GROUP * (s + 1), :].astype(jnp.float32))
            return carry

        def load_other(r, carry):
            for s in range(low):
                put(rows - 1 - r, s, x_other[r, GROUP * s : GROUP * (s + 1), :].astype(jnp.float32))
            return carry

        if near:
            cols = GROUP * low
            totals = spread_pixels(pix, by_col, vecs, diagonal, spread, ready)
            for n in range(rows):
                total = totals[n % len(totals)]
                to = n + core * (rows - 1 - 2 * n)
                for s in range(low):
                    at = (n // len(totals)) * cols + GROUP * s
                    put(to, s, total[at : at + GROUP])
        else:
            lax.fori_loop(0, x_own.shape[0], load_row, 0)
            lax.fori_loop(0, x_other.shape[0], load_other, 0)

        for b in range(blocks):
            kept = rows - 2 * (b + 1)
            ub = vecs[b, 0:1, :]
            gain = vecs[b, 1:2, 0:width]
            shift = vecs[b, 2:3, 0:width]

            def conv_rows(n, carry, b=b):
                t = n // chunks
                chunk = n % chunks
                lanes = pl.ds(pl.multiple_of(chunk * 128, 128), 128)
                sums = [[None] * low for _ in range(2)]

                def line(r):
                    return [
                        xpad[chunk, 2 * t + r, s].astype(jnp.bfloat16) for s in range(low + 4)
                    ]

                window = [line(0)]
                for i in range(5):
                    window = [*window[-1:], line(i + 1)]
                    tap = []
                    for j in range(5):
                        w = taps[b, chunk, 5 * i + j]
                        tap.append(jnp.concatenate([w, w], axis=0).astype(jnp.bfloat16))
                    for o in range(2):
                        for s in range(low):
                            part = window[o][s] * tap[0]
                            for j in range(1, 5):
                                part = part + window[o][s + j] * tap[j]
                            sums[o][s] = part if i == 0 else sums[o][s] + part
                for o in range(2):
                    for s in range(low):
                        at = pl.multiple_of(((2 * t + o) * low + s) * GROUP, GROUP)
                        acc[pl.ds(at, GROUP), lanes] = sums[o][s].astype(jnp.float32)
                return carry

            lax.fori_loop(0, kept // 2 * chunks, conv_rows, 0, unroll=UNROLL)
            part = kept * low * GROUP // 2

            def norm_rows(t, gain=gain, part=part):
                at = pl.ds(pl.multiple_of(t * part, part), part)
                v = acc[at, :]
                d = v - jnp.mean(v, axis=-1, keepdims=True)
                spread = jnp.mean(d * d, axis=-1, keepdims=True)
                normed[at, :] = (d * lax.rsqrt(spread + EPSILON) * gain).astype(jnp.bfloat16)

            norm_rows(0)
            weights_in(b)

            for t in range(2):
                at = slice(t * part, (t + 1) * part)
                nv = normed[at, :]
                if t == 0:
                    norm_rows(1)
                else:
                    lay(b + 1)
                parts = []
                for n in range(hid // tile):
                    cut = slice(n * tile, (n + 1) * tile)
                    h = jnp.dot(nv, up[b, :, cut], preferred_element_type=jnp.float32)
                    h = h + ub[:, cut]
                    parts.append((0.5 * h * (1.0 + lax.erf(h * (2.0**-0.5)))).astype(jnp.bfloat16))
                branch = jnp.dot(
                    jnp.concatenate(parts, axis=1), dn[b], preferred_element_type=jnp.float32
                )
                for r in range(kept // 2):
                    row = t * (kept // 2) + r
                    for s in range(low):
                        lines = slice((r * low + s) * GROUP, (r * low + s + 1) * GROUP)
                        v = held(row, s) + branch[lines] + shift
                        if b + 1 < blocks:
                            put(row, s, v)
                        else:
                            to = row if near else 2 * jnp.bitwise_xor(row // 2, level) + row % 2
                            out[to, GROUP * s : GROUP * (s + 1), :] = v.astype(out.dtype)


def placed(x):
    return pltpu.with_memory_space_constraint(x, pltpu.VMEM)


def kept_out(x):
    return pltpu.with_memory_space_constraint(x, pltpu.HBM)


def stage(kind, xs, cols, weights):
    first, near = kind == "first", kind != "far"
    rows = 2 * xs[0].shape[0]
    if first:
        half, width, hid = weights[4].shape
        blocks = 2 * half
    else:
        blocks, width, hid = weights[0].shape
    kept = rows - 2 * blocks
    low = cols // GROUP
    vmem = pl.BlockSpec(memory_space=pltpu.VMEM)
    hbm = pl.BlockSpec(memory_space=pltpu.HBM)
    work = (rows * blocks - blocks * (blocks + 1)) * cols
    outs = [pltpu.VMEM((kept, cols, width), jnp.bfloat16)]
    scratch = [
        pltpu.VMEM((width // 128, rows + 2, low + 4, GROUP, 128), jnp.float32),
        pltpu.VMEM((rows * cols, width), jnp.bfloat16),
        pltpu.VMEM((rows * cols, width), jnp.float32),
    ]
    if near:
        bands, variables, lines, wide = xs[0].shape
        depth = PATCH * variables * lines
        scratch += [
            pltpu.VMEM((2, depth, PATCH * wide), jnp.bfloat16),
            pltpu.VMEM((bands * cols, depth), jnp.bfloat16),
        ]
    if first:
        outs += [
            pltpu.VMEM((blocks, width, hid), jnp.bfloat16),
            pltpu.VMEM((blocks, hid, width), jnp.bfloat16),
            pltpu.VMEM((blocks, width // 128, 25, 8, 128), jnp.float32),
            pltpu.VMEM((blocks, 8, hid), jnp.float32),
            pltpu.VMEM((lines // PATCH, depth, width), jnp.bfloat16),
        ]
        small = [*weights[:4], *weights[6:10], *weights[12:]]
        scratch += [pltpu.VMEM(w.shape, w.dtype) for w in small]
        scratch += [pltpu.SemaphoreType.DMA((3, max(blocks, len(small))))]
    stays = [first and n != 10 for n in range(len(weights))]
    operands = [placed(x) for x in xs]
    operands += [kept_out(w) if stay else placed(w) for w, stay in zip(weights, stays)]
    return pl.pallas_call(
        functools.partial(stage_kernel, rows, kind),
        out_shape=tuple(outs),
        in_specs=[vmem] * len(xs) + [hbm if stay else vmem for stay in stays],
        out_specs=(vmem,) * len(outs),
        scratch_shapes=scratch,
        compiler_params=pltpu.CompilerParams(vmem_limit_bytes=VMEM_LIMIT),
        cost_estimate=pl.CostEstimate(
            flops=8 * work * width * hid,
            bytes_accessed=4 * blocks * width * hid,
            transcendentals=work * hid,
        ),
        name=kind + "_stage",
    )(*operands)


def choose_kernel(home, last, *pieces):
    rows = pieces[0].shape[0]
    near = lax.axis_index("segment") // 2 == 0
    for flag, source in ((near, home), (jnp.logical_not(near), last)):

        @pl.when(flag)
        def _():
            for t, piece in enumerate(pieces):
                piece[...] = source[t * rows : (t + 1) * rows]


def choose(home, last, count):
    vmem = pl.BlockSpec(memory_space=pltpu.VMEM)
    rows, cols, width = last.shape
    return pl.pallas_call(
        choose_kernel,
        out_shape=(pltpu.VMEM((rows // count, cols, width), last.dtype),) * count,
        in_specs=[vmem] * 2,
        out_specs=(vmem,) * count,
        compiler_params=pltpu.CompilerParams(vmem_limit_bytes=VMEM_LIMIT),
        cost_estimate=pl.CostEstimate(flops=0, bytes_accessed=4 * last.size, transcendentals=0),
        name="choose",
    )(placed(home), placed(last))


def project(x, gain, memory_weight):
    v = x[...].reshape(-1, x.shape[-1]).astype(jnp.float32)
    d = v - jnp.mean(v, axis=-1, keepdims=True)
    spread = jnp.mean(d * d, axis=-1, keepdims=True)
    n = (d * lax.rsqrt(spread + EPSILON) * gain[...].astype(jnp.float32)).astype(jnp.bfloat16)
    return jnp.dot(n, memory_weight[...], preferred_element_type=jnp.float32).astype(jnp.bfloat16)


def project_kernel(*refs):
    *xs, gain, memory_weight, kv = refs
    for i, x in enumerate(xs):
        kv[i] = project(x, gain, memory_weight)


def fold_kernel(before, x, gain, latents, memory_weight, output_weight, out, last, mixed, shown):
    rows, cols, width = x.shape
    levels = before.shape[0] + 1
    places = rows * cols
    low = cols // GROUP
    scale = HSZ**-0.5
    last[...] = project(x, gain, memory_weight)
    kv = [before.at[i] for i in range(levels - 1)] + [last]
    lat = latents[...].astype(jnp.float32)
    pairs = NLAT * HEADS
    at_row = lax.broadcasted_iota(jnp.int32, (pairs, width), 0)
    at_col = lax.broadcasted_iota(jnp.int32, (pairs, width), 1)
    head = at_col // HSZ == at_row % HEADS
    wide = jnp.concatenate(
        [jnp.broadcast_to(lat[q : q + 1], (HEADS, width)) for q in range(NLAT)], axis=0
    )
    queries = jnp.where(head, wide, 0.0).astype(jnp.bfloat16)
    raised = []
    for i in range(levels):
        s = lax.dot_general(
            kv[i][:, :width],
            queries,
            (((1,), (1,)), ((), ())),
            preferred_element_type=jnp.float32,
        )
        raised.append(jnp.exp(s * scale))
    total = raised[0]
    for i in range(1, levels):
        total = total + raised[i]
    shares = [(r / total).astype(jnp.bfloat16) for r in raised]
    for q in range(NLAT):
        pick = jnp.where(jnp.logical_and(head, at_row // HEADS == q), 1.0, 0.0).astype(jnp.bfloat16)
        m = None
        for i in range(levels):
            w = jnp.dot(shares[i], pick, preferred_element_type=jnp.float32)
            term = w * kv[i][:, width:].astype(jnp.float32)
            m = term if m is None else m + term
        mixed[q * places : (q + 1) * places, :] = m.astype(jnp.bfloat16)
    folded = jnp.dot(mixed[...], output_weight[...], preferred_element_type=jnp.float32)
    flip = (lax.axis_index("lat") >= levels).astype(jnp.int32)
    for q in range(NLAT):
        for r in range(rows):
            for s in range(cols // 8):
                at = q * places + r * cols + 8 * s
                row = r + flip * (rows - 1 - 2 * r)
                group, first = divmod(8 * s, GROUP)
                start = (row * NLAT + q) * cols + first * low + group
                for lane in range(0, width, 128):
                    shown[lane // 128, pl.ds(start, 8, stride=low), :] = (
                        folded[at : at + 8, lane : lane + 128] + lat[q : q + 1, lane : lane + 128]
                    )
    for lane in range(0, width, 128):
        v = shown[lane // 128].astype(out.dtype)
        out[:, :, :, lane : lane + 128] = v.reshape(rows, NLAT, cols, 128)


def fold(xs, gain, latents, memory_weight, output_weight):
    rows, cols, width = xs[0].shape
    places = rows * cols
    vmem = pl.BlockSpec(memory_space=pltpu.VMEM)
    params = pltpu.CompilerParams(vmem_limit_bytes=VMEM_LIMIT)
    gain, latents, memory_weight, output_weight = map(
        placed, (gain, latents, memory_weight, output_weight)
    )
    *early, late = map(placed, xs)
    before = pl.pallas_call(
        project_kernel,
        out_shape=pltpu.VMEM((len(early), places, 2 * width), jnp.bfloat16),
        in_specs=[vmem] * (len(early) + 2),
        out_specs=vmem,
        compiler_params=params,
        cost_estimate=pl.CostEstimate(
            flops=4 * len(early) * places * width * width,
            bytes_accessed=2_000_000,
            transcendentals=0,
        ),
        name="project",
    )(*early, gain, memory_weight)
    return pl.pallas_call(
        fold_kernel,
        out_shape=jax.ShapeDtypeStruct((rows, NLAT, cols, width), jnp.bfloat16),
        in_specs=[vmem] * 6,
        out_specs=vmem,
        scratch_shapes=[
            pltpu.VMEM((places, 2 * width), jnp.bfloat16),
            pltpu.VMEM((NLAT * places, width), jnp.bfloat16),
            pltpu.VMEM((width // 128, NLAT * places, 128), jnp.float32),
        ],
        compiler_params=params,
        cost_estimate=pl.CostEstimate(
            flops=8 * places * width * width, bytes_accessed=2_000_000, transcendentals=0
        ),
        name="fold",
    )(placed(before), late, gain, latents, memory_weight, output_weight)


def fits(mesh, shapes):
    pixels, embed_weight, depth, up = shapes[0], shapes[1], shapes[3], shapes[5]
    micro, levels, _, height, wide = pixels
    lat, segment = mesh.shape["lat"], mesh.shape["segment"]
    rows, cols = height // PATCH, wide // PATCH
    blocks = depth[0] // 2 * depth[1]
    return (
        segment == 4
        and depth[0] == segment
        and micro == segment
        and micro * levels == 2 * lat
        and rows == 2 * lat
        and rows == 4 * blocks
        and cols % 32 == 0
        and wide == 128
        and lat == 2 * levels
        and levels & (levels - 1) == 0
        and up[2] % 256 == 0
        and embed_weight[1] % 256 == 0
    )


def on_columns(
    pixels,
    embed_weight,
    level_code,
    depth_kernel,
    norm_gain,
    up_weight,
    up_bias,
    down_weight,
    down_bias,
    fold_gain,
    latents,
    memory_weight,
    output_weight,
):
    lat = lax.axis_size("lat")
    micro, levels, variables, height, wide = pixels.shape
    cols = wide // PATCH
    width = embed_weight.shape[1]

    swap = [(0, 1), (1, 0), (2, 3), (3, 2)]
    own = (depth_kernel[0].transpose(1, 0, 2), norm_gain[0], up_bias[0], down_bias[0])
    own = (*own, up_weight[0], down_weight[0])
    oth = tuple(lax.ppermute(w, "segment", swap) for w in own)
    got = lax.all_to_all(
        pixels.reshape(2, lat, variables, height, wide), "lat", 1, 1, tiled=True
    )

    got, oth = lax.optimization_barrier((got, oth))

    onward = [(0, 2), (1, 3)]
    across = [(2, 3), (3, 2)]
    sent = []
    for i in range(2):
        if i == 0:
            a, *weights, by_col = stage("first", (got[i],), cols, (*own, *oth, embed_weight, level_code))
        else:
            (a,) = stage("near", (got[i], by_col), cols, weights)
            a, sent[0] = lax.optimization_barrier((a, sent[0]))
        sent.append(lax.ppermute(a, "segment", onward))
    done = []
    for i in range(2):
        if i:
            done[0], sent[i] = lax.optimization_barrier((done[0], sent[i]))
        other = lax.ppermute(sent[i], "segment", across)
        (a,) = stage("far", (sent[i], other), cols, weights)
        done.append(a)
    home = lax.ppermute(done[0], "segment", [(j, i) for i, j in onward])

    pieces = []
    leaving = choose(home, done[1], levels)
    for t in range(levels):
        pairs = []
        for s in range(4):
            for l in range(lat):
                k = (l % levels) ^ t
                to_lat = k if s % 2 == 0 else lat - 1 - k
                to_seg = 2 * (s // 2) + l // levels
                pairs.append((s * lat + l, to_seg * lat + to_lat))
        pieces.append(lax.ppermute(leaving[t], ("segment", "lat"), pairs))
    folded = fold(pieces, fold_gain[None, :], latents, memory_weight, output_weight)
    return folded.transpose(0, 2, 1, 3)[None]


def solution(mesh):
    specs = (
        P(None, None, None, "lat", None),
        P(),
        P(),
        P("segment", None, None, None),
        P("segment", None, None),
        P("segment", None, None, None),
        P("segment", None, None),
        P("segment", None, None, None),
        P("segment", None, None),
        P(),
        P(),
        P(),
        P(),
    )

    def program(*arrays):
        body = on_columns if fits(mesh, [a.shape for a in arrays]) else on_device

        return jax.shard_map(
            body,
            mesh=mesh,
            in_specs=specs,
            out_specs=P("segment", "lat", None, None, None),
            check_vma=False,
        )(*arrays)

    return program
```

```python
import functools

import jax
import jax.numpy as jnp
from jax import lax
from jax.experimental import pallas as pl
from jax.experimental.pallas import tpu as pltpu
from jax.sharding import PartitionSpec as P

HEADS = 16
HSZ = 32
PATCH = 4
NLAT = 3
BLOCKS = 2


EPSILON = 1e-06


VMEM_LIMIT = 16 * 1024 * 1024
GROUP = 16
UNROLL = 4

def extended(x, sides, width):
    for axis, dim in sides:
        size, length = (lax.axis_size(axis), x.shape[dim])
        up = [(i, (i + 1) % size) for i in range(size - 1)]
        down = [(j, i) for i, j in up]
        last = lax.slice_in_dim(x, length - width, length, axis=dim)
        first = lax.slice_in_dim(x, 0, width, axis=dim)
        before = lax.ppermute(last, axis, up)
        after = lax.ppermute(first, axis, down)
        x = jnp.concatenate([before, x, after], axis=dim)
    return x


def normalize(values_in, gain):
    average = jnp.mean(values_in, axis=-1, keepdims=True)
    centred = values_in - average
    spread_sq = jnp.mean(centred * centred, axis=-1, keepdims=True)
    return centred * lax.rsqrt(spread_sq + EPSILON) * gain.astype(jnp.float32)


def depthwise(padded, kernel, row_count, col_count):
    conv_out = jnp.zeros((padded.shape[0], row_count, col_count, padded.shape[3]), jnp.float32)
    for row_off in range(5):
        for col_off in range(5):
            window = padded[
                :, row_off : row_off + row_count, col_off : col_off + col_count, :
            ].astype(jnp.float32)
            conv_out = conv_out + window * kernel[row_off * 5 + col_off].astype(jnp.float32)
    return conv_out


def conv_block(features, padded_rows, kernel, gain, up_mat, up_shift, down_mat, down_shift):
    padded = jnp.pad(padded_rows, ((0, 0), (0, 0), (2, 2), (0, 0)))
    row_count = features.shape[1]
    col_count = features.shape[2]
    width = features.shape[3]
    conv_out = depthwise(padded, kernel, row_count, col_count)
    normed = normalize(conv_out, gain).astype(jnp.bfloat16)
    flat_rows = normed.reshape(-1, width)
    hidden = jax.nn.gelu(
        jnp.dot(flat_rows, up_mat, preferred_element_type=jnp.float32)
        + up_shift.astype(jnp.float32),
        approximate=False,
    ).astype(jnp.bfloat16)
    branch = jnp.dot(hidden, down_mat, preferred_element_type=jnp.float32) + down_shift.astype(
        jnp.float32
    )
    return (features.astype(jnp.float32) + branch.reshape(features.shape)).astype(jnp.bfloat16)


def embed_patches(sample_pixels, embed_weight, level_code):
    levels = sample_pixels.shape[0]
    variables = sample_pixels.shape[1]
    row_count = sample_pixels.shape[2] // PATCH
    col_count = sample_pixels.shape[3] // PATCH
    patches = sample_pixels.reshape(levels, variables, row_count, PATCH, col_count, PATCH)
    patches = patches.transpose(0, 2, 4, 1, 3, 5).reshape(
        levels * row_count * col_count, variables * PATCH * PATCH
    )
    embedded = jnp.dot(patches, embed_weight, preferred_element_type=jnp.float32).reshape(
        levels, row_count, col_count, -1
    )
    embedded = embedded + level_code[:, None, None, :].astype(jnp.float32)
    return embedded.astype(jnp.bfloat16)


def fold_levels(features, fold_gain, latents, memory_weight, output_weight):
    levels, row_count, col_count, width = features.shape
    places = row_count * col_count
    normed = (
        normalize(features.astype(jnp.float32), fold_gain)
        .astype(jnp.bfloat16)
        .reshape(levels * places, width)
    )
    keyval = jnp.dot(normed, memory_weight, preferred_element_type=jnp.float32).astype(jnp.bfloat16)
    keyval = keyval.reshape(levels, places, 2, HEADS, HSZ)
    queries = latents.reshape(NLAT, HEADS, HSZ)
    scores = jnp.einsum(
        "lphe,qhe->pqlh", keyval[:, :, 0], queries, preferred_element_type=jnp.float32
    ) * HSZ ** (-0.5)
    raised = jnp.exp(scores)
    share = (raised / jnp.sum(raised, axis=2, keepdims=True)).astype(jnp.bfloat16)
    mixed = jnp.einsum(
        "pqlh,lphe->pqhe", share, keyval[:, :, 1], preferred_element_type=jnp.float32
    )
    mixed = mixed.astype(jnp.bfloat16).reshape(places * NLAT, width)
    folded = jnp.dot(mixed, output_weight, preferred_element_type=jnp.float32).reshape(
        places, NLAT, width
    )
    folded = folded + latents.astype(jnp.float32)[None, :, :]
    return folded.astype(jnp.bfloat16).reshape(row_count, col_count, NLAT, width)


def run_section(features, section_weights):
    for block_id in range(BLOCKS):
        padded_rows = extended(features, (("lat", 1),), 2)
        features = conv_block(
            features,
            padded_rows,
            section_weights[0][block_id],
            section_weights[1][block_id],
            section_weights[2][block_id],
            section_weights[3][block_id],
            section_weights[4][block_id],
            section_weights[5][block_id],
        )
    return features


def on_device(
    pixels,
    embed_weight,
    level_code,
    depth_kernel,
    norm_gain,
    up_weight,
    up_bias,
    down_weight,
    down_bias,
    fold_gain,
    latents,
    memory_weight,
    output_weight,
):
    segment_index = lax.axis_index("segment")
    sections = lax.axis_size("segment")
    count_all = pixels.shape[0]
    per_segment = count_all // sections

    def fold_one(features):
        return fold_levels(features, fold_gain, latents, memory_weight, output_weight)

    all_weights = (
        lax.all_gather(depth_kernel, "segment", axis=0, tiled=True),
        lax.all_gather(norm_gain, "segment", axis=0, tiled=True),
        lax.all_gather(up_weight, "segment", axis=0, tiled=True),
        lax.all_gather(up_bias, "segment", axis=0, tiled=True),
        lax.all_gather(down_weight, "segment", axis=0, tiled=True),
        lax.all_gather(down_bias, "segment", axis=0, tiled=True),
    )
    own_pixels = lax.dynamic_slice_in_dim(pixels, segment_index * per_segment, per_segment, 0)

    def per_sample(sample_pixels):
        features = embed_patches(sample_pixels, embed_weight, level_code)
        for section_id in range(sections):
            features = run_section(
                features, tuple((weight_set[section_id] for weight_set in all_weights))
            )
        return fold_one(features)

    return lax.map(per_sample, own_pixels)


def spread_pixels(pix, by_col, vecs, diagonal, spread, ready):
    bands, variables, lines, wide = pix.shape
    cols = wide // PATCH
    low = cols // GROUP
    taken = variables * lines
    at = lax.broadcasted_iota(jnp.int32, (cols, PATCH * wide), 1)
    spot = lax.broadcasted_iota(jnp.int32, (cols, PATCH * wide), 0)
    source = ((spot % GROUP) * low + spot // GROUP) * PATCH + at // wide
    pick = jnp.where(source == at % wide, 1.0, 0.0).astype(jnp.bfloat16)
    for slot in range(2):
        diagonal[slot] = jnp.zeros(diagonal.shape[1:], diagonal.dtype)
    for n in range(bands):
        slot = n % 2
        for p in range(PATCH):
            diagonal[slot, p * taken : (p + 1) * taken, p * wide : (p + 1) * wide] = pix[n].reshape(
                taken, wide
            )
        spread[n * cols : (n + 1) * cols, :] = lax.dot_general(
            pick, diagonal[slot], (((1,), (1,)), ((), ())), preferred_element_type=jnp.float32
        ).astype(jnp.bfloat16)
    ready()
    code = vecs[0, 3:4, 0 : by_col.shape[-1]]
    return [
        jnp.dot(spread[...], by_col[b], preferred_element_type=jnp.float32) + code
        for b in range(by_col.shape[0])
    ]


def lay_block(b, core, own, oth, taps, vecs):
    depth, gain, ub, db = range(4)
    half, width = own[db].shape
    line = slice(b % half, b % half + 1)

    def chosen(n, even, odd, b=b):
        a, c = (own[n], oth[n]) if b < half else (oth[n], own[n])
        return jnp.where(core == 1, c[odd].astype(jnp.float32), a[even].astype(jnp.float32))

    for i in range(5):
        for j in range(5):
            p, q = 5 * i + j, 5 * (4 - i) + j
            tap = chosen(depth, (p, line), (q, line))
            for n in range(width // 128):
                taps[b, n, p] = jnp.broadcast_to(tap[:, 128 * n : 128 * (n + 1)], (8, 128))
    at = (line, slice(None))
    vecs[b, 0:1, :] = chosen(ub, at, at)
    vecs[b, 1:2, 0:width] = chosen(gain, at, at)
    vecs[b, 2:3, 0:width] = chosen(db, at, at)


def lay_shared(level, lines, weight, code, vecs, by_col):
    width = weight.shape[1]
    shown = code[0:1, :].astype(jnp.float32)
    for n in range(1, code.shape[0]):
        shown = jnp.where(level == n, code[n : n + 1, :].astype(jnp.float32), shown)
    vecs[0, 3:4, 0:width] = shown
    deep = weight.shape[0]
    taken = deep // (PATCH * PATCH) * lines
    row = lax.broadcasted_iota(jnp.int32, (PATCH * taken, deep), 0)
    source = lax.broadcasted_iota(jnp.int32, (PATCH * taken, deep), 1)
    to = row % taken
    base = (to // lines) * (PATCH * PATCH) + (to % PATCH) * PATCH + row // taken
    for b in range(lines // PATCH):
        same = jnp.logical_and(base == source, (to % lines) // PATCH == b)
        by_col[b] = jnp.dot(
            jnp.where(same, 1.0, 0.0).astype(jnp.bfloat16),
            weight[...],
            preferred_element_type=jnp.float32,
        ).astype(jnp.bfloat16)


def stage_kernel(rows, kind, *refs):
    first, near = kind == "first", kind != "far"
    if first:
        pix, *stored = refs[:15]
        out, up, dn, taps, vecs, by_col, xpad, normed, acc, diagonal, spread, *held_small, sems = refs[15:]
    elif near:
        pix, by_col, up, dn, taps, vecs, out, xpad, normed, acc, diagonal, spread = refs
    else:
        x_own, x_other, up, dn, taps, vecs, out, xpad, normed, acc = refs
    segment = lax.axis_index("segment")
    place = lax.axis_index("lat")
    width = out.shape[-1]
    blocks, _, hid = up.shape
    low = out.shape[1] // GROUP
    core = lax.rem(segment, 2)
    level = lax.rem(place, out.shape[0] // 2)
    tile = 256
    chunks = width // 128


    def put(r, s, v):
        group = lax.broadcasted_iota(jnp.int32, (GROUP, 128), 0)
        for n in range(chunks):
            part = v[:, 128 * n : 128 * (n + 1)]
            xpad[n, r + 2, s + 2] = part
            for d in (-2, -1, low, low + 1):
                if d % low == s:
                    by = -(d // low)
                    edge = 0 if by > 0 else GROUP - 1
                    moved = pltpu.roll(part, by % GROUP, 0)
                    xpad[n, r + 2, d + 2] = jnp.where(group == edge, 0.0, moved)

    def held(r, s):
        return jnp.concatenate([xpad[n, r + 2, s + 2] for n in range(chunks)], axis=1)

    active = segment // 2 == (0 if near else 1)
    if first:
        half = blocks // 2
        own, oth = stored[:6], stored[6:12]
        small = [*own[:4], *oth[:4], *stored[12:]]
        arrivals = [
            pltpu.make_async_copy(a, b, sems.at[2, n]) for n, (a, b) in enumerate(zip(small, held_small))
        ]
        for copy in arrivals:
            copy.start()
        for k in range(half):
            for source, start in ((own, core * half), (oth, (1 - core) * half)):
                pltpu.make_async_copy(source[4].at[k], up.at[start + k], sems.at[0, start + k]).start()
                pltpu.make_async_copy(source[5].at[k], dn.at[start + k], sems.at[1, start + k]).start()

    def lay(b):
        if first and b < blocks:
            lay_block(b, core, held_small[:4], held_small[4:8], taps, vecs)

    def ready():
        if first:
            for copy in arrivals:
                copy.wait()
            lay_shared(level, pix.shape[2], *held_small[8:], vecs, by_col)
            lay(0)

    def weights_in(b):
        if first:
            k = b % (blocks // 2)
            pltpu.make_async_copy(stored[4].at[k], up.at[b], sems.at[0, b]).wait()
            pltpu.make_async_copy(stored[5].at[k], dn.at[b], sems.at[1, b]).wait()

    @pl.when(jnp.logical_not(active))
    def _():
        ready()
        for b in range(blocks):
            if b:
                lay(b)
            weights_in(b)

    @pl.when(active)
    def _():
        zero = jnp.zeros((GROUP, 128), xpad.dtype)
        for n in range(chunks):
            for r in range(2):
                for s in range(low + 4):
                    xpad[n, r, s] = zero

        def load_row(r, carry):
            for s in range(low):
                put(r, s, x_own[r, GROUP * s : GROUP * (s + 1), :].astype(jnp.float32))
            return carry

        def load_other(r, carry):
            for s in range(low):
                put(rows - 1 - r, s, x_other[r, GROUP * s : GROUP * (s + 1), :].astype(jnp.float32))
            return carry

        if near:
            cols = GROUP * low
            totals = spread_pixels(pix, by_col, vecs, diagonal, spread, ready)
            for n in range(rows):
                total = totals[n % len(totals)]
                to = n + core * (rows - 1 - 2 * n)
                for s in range(low):
                    at = (n // len(totals)) * cols + GROUP * s
                    put(to, s, total[at : at + GROUP])
        else:
            lax.fori_loop(0, x_own.shape[0], load_row, 0)
            lax.fori_loop(0, x_other.shape[0], load_other, 0)

        for b in range(blocks):
            kept = rows - 2 * (b + 1)
            ub = vecs[b, 0:1, :]
            gain = vecs[b, 1:2, 0:width]
            shift = vecs[b, 2:3, 0:width]

            def conv_rows(n, carry, b=b):
                t = n // chunks
                chunk = n % chunks
                lanes = pl.ds(pl.multiple_of(chunk * 128, 128), 128)
                sums = [[None] * low for _ in range(2)]

                def line(r):
                    return [
                        xpad[chunk, 2 * t + r, s].astype(jnp.bfloat16) for s in range(low + 4)
                    ]

                window = [line(0)]
                for i in range(5):
                    window = [*window[-1:], line(i + 1)]
                    tap = []
                    for j in range(5):
                        w = taps[b, chunk, 5 * i + j]
                        tap.append(jnp.concatenate([w, w], axis=0).astype(jnp.bfloat16))
                    for o in range(2):
                        for s in range(low):
                            part = window[o][s] * tap[0]
                            for j in range(1, 5):
                                part = part + window[o][s + j] * tap[j]
                            sums[o][s] = part if i == 0 else sums[o][s] + part
                for o in range(2):
                    for s in range(low):
                        at = pl.multiple_of(((2 * t + o) * low + s) * GROUP, GROUP)
                        acc[pl.ds(at, GROUP), lanes] = sums[o][s].astype(jnp.float32)
                return carry

            lax.fori_loop(0, kept // 2 * chunks, conv_rows, 0, unroll=UNROLL)
            part = kept * low * GROUP // 2

            def norm_rows(t, gain=gain, part=part):
                at = pl.ds(pl.multiple_of(t * part, part), part)
                v = acc[at, :]
                d = v - jnp.mean(v, axis=-1, keepdims=True)
                spread = jnp.mean(d * d, axis=-1, keepdims=True)
                normed[at, :] = (d * lax.rsqrt(spread + EPSILON) * gain).astype(jnp.bfloat16)

            norm_rows(0)
            weights_in(b)

            for t in range(2):
                at = slice(t * part, (t + 1) * part)
                nv = normed[at, :]
                if t == 0:
                    norm_rows(1)
                else:
                    lay(b + 1)
                parts = []
                for n in range(hid // tile):
                    cut = slice(n * tile, (n + 1) * tile)
                    h = jnp.dot(nv, up[b, :, cut], preferred_element_type=jnp.float32)
                    h = h + ub[:, cut]
                    parts.append((0.5 * h * (1.0 + lax.erf(h * (2.0**-0.5)))).astype(jnp.bfloat16))
                branch = jnp.dot(
                    jnp.concatenate(parts, axis=1), dn[b], preferred_element_type=jnp.float32
                )
                for r in range(kept // 2):
                    row = t * (kept // 2) + r
                    for s in range(low):
                        lines = slice((r * low + s) * GROUP, (r * low + s + 1) * GROUP)
                        v = held(row, s) + branch[lines] + shift
                        if b + 1 < blocks:
                            put(row, s, v)
                        else:
                            to = row if near else 2 * jnp.bitwise_xor(row // 2, level) + row % 2
                            out[to, GROUP * s : GROUP * (s + 1), :] = v.astype(out.dtype)


def placed(x):
    return pltpu.with_memory_space_constraint(x, pltpu.VMEM)


def kept_out(x):
    return pltpu.with_memory_space_constraint(x, pltpu.HBM)


def stage(kind, xs, cols, weights):
    first, near = kind == "first", kind != "far"
    rows = 2 * xs[0].shape[0]
    if first:
        half, width, hid = weights[4].shape
        blocks = 2 * half
    else:
        blocks, width, hid = weights[0].shape
    kept = rows - 2 * blocks
    low = cols // GROUP
    vmem = pl.BlockSpec(memory_space=pltpu.VMEM)
    hbm = pl.BlockSpec(memory_space=pltpu.HBM)
    work = (rows * blocks - blocks * (blocks + 1)) * cols
    outs = [pltpu.VMEM((kept, cols, width), jnp.bfloat16)]
    scratch = [
        pltpu.VMEM((width // 128, rows + 2, low + 4, GROUP, 128), jnp.float32),
        pltpu.VMEM((rows * cols, width), jnp.bfloat16),
        pltpu.VMEM((rows * cols, width), jnp.float32),
    ]
    if near:
        bands, variables, lines, wide = xs[0].shape
        depth = PATCH * variables * lines
        scratch += [
            pltpu.VMEM((2, depth, PATCH * wide), jnp.bfloat16),
            pltpu.VMEM((bands * cols, depth), jnp.bfloat16),
        ]
    if first:
        outs += [
            pltpu.VMEM((blocks, width, hid), jnp.bfloat16),
            pltpu.VMEM((blocks, hid, width), jnp.bfloat16),
            pltpu.VMEM((blocks, width // 128, 25, 8, 128), jnp.float32),
            pltpu.VMEM((blocks, 8, hid), jnp.float32),
            pltpu.VMEM((lines // PATCH, depth, width), jnp.bfloat16),
        ]
        small = [*weights[:4], *weights[6:10], *weights[12:]]
        scratch += [pltpu.VMEM(w.shape, w.dtype) for w in small]
        scratch += [pltpu.SemaphoreType.DMA((3, max(blocks, len(small))))]
    stays = [first and n != 10 for n in range(len(weights))]
    operands = [placed(x) for x in xs]
    operands += [kept_out(w) if stay else placed(w) for w, stay in zip(weights, stays)]
    return pl.pallas_call(
        functools.partial(stage_kernel, rows, kind),
        out_shape=tuple(outs),
        in_specs=[vmem] * len(xs) + [hbm if stay else vmem for stay in stays],
        out_specs=(vmem,) * len(outs),
        scratch_shapes=scratch,
        compiler_params=pltpu.CompilerParams(vmem_limit_bytes=VMEM_LIMIT),
        cost_estimate=pl.CostEstimate(
            flops=8 * work * width * hid,
            bytes_accessed=4 * blocks * width * hid,
            transcendentals=work * hid,
        ),
        name=kind + "_stage",
    )(*operands)


def choose_kernel(home, last, *pieces):
    rows = pieces[0].shape[0]
    near = lax.axis_index("segment") // 2 == 0
    for flag, source in ((near, home), (jnp.logical_not(near), last)):

        @pl.when(flag)
        def _():
            for t, piece in enumerate(pieces):
                piece[...] = source[t * rows : (t + 1) * rows]


def choose(home, last, count):
    vmem = pl.BlockSpec(memory_space=pltpu.VMEM)
    rows, cols, width = last.shape
    return pl.pallas_call(
        choose_kernel,
        out_shape=(pltpu.VMEM((rows // count, cols, width), last.dtype),) * count,
        in_specs=[vmem] * 2,
        out_specs=(vmem,) * count,
        compiler_params=pltpu.CompilerParams(vmem_limit_bytes=VMEM_LIMIT),
        cost_estimate=pl.CostEstimate(flops=0, bytes_accessed=4 * last.size, transcendentals=0),
        name="choose",
    )(placed(home), placed(last))


def project(x, gain, memory_weight):
    v = x[...].reshape(-1, x.shape[-1]).astype(jnp.float32)
    d = v - jnp.mean(v, axis=-1, keepdims=True)
    spread = jnp.mean(d * d, axis=-1, keepdims=True)
    n = (d * lax.rsqrt(spread + EPSILON) * gain[...].astype(jnp.float32)).astype(jnp.bfloat16)
    return jnp.dot(n, memory_weight[...], preferred_element_type=jnp.float32).astype(jnp.bfloat16)


def project_kernel(*refs):
    *xs, gain, memory_weight, kv = refs
    for i, x in enumerate(xs):
        kv[i] = project(x, gain, memory_weight)


def fold_kernel(before, x, gain, latents, memory_weight, output_weight, out, last, mixed, shown):
    rows, cols, width = x.shape
    levels = before.shape[0] + 1
    places = rows * cols
    low = cols // GROUP
    scale = HSZ**-0.5
    last[...] = project(x, gain, memory_weight)
    kv = [before.at[i] for i in range(levels - 1)] + [last]
    lat = latents[...].astype(jnp.float32)
    pairs = NLAT * HEADS
    at_row = lax.broadcasted_iota(jnp.int32, (pairs, width), 0)
    at_col = lax.broadcasted_iota(jnp.int32, (pairs, width), 1)
    head = at_col // HSZ == at_row % HEADS
    wide = jnp.concatenate(
        [jnp.broadcast_to(lat[q : q + 1], (HEADS, width)) for q in range(NLAT)], axis=0
    )
    queries = jnp.where(head, wide, 0.0).astype(jnp.bfloat16)
    raised = []
    for i in range(levels):
        s = lax.dot_general(
            kv[i][:, :width],
            queries,
            (((1,), (1,)), ((), ())),
            preferred_element_type=jnp.float32,
        )
        raised.append(jnp.exp(s * scale))
    total = raised[0]
    for i in range(1, levels):
        total = total + raised[i]
    shares = [(r / total).astype(jnp.bfloat16) for r in raised]
    for q in range(NLAT):
        pick = jnp.where(jnp.logical_and(head, at_row // HEADS == q), 1.0, 0.0).astype(jnp.bfloat16)
        m = None
        for i in range(levels):
            w = jnp.dot(shares[i], pick, preferred_element_type=jnp.float32)
            term = w * kv[i][:, width:].astype(jnp.float32)
            m = term if m is None else m + term
        mixed[q * places : (q + 1) * places, :] = m.astype(jnp.bfloat16)
    folded = jnp.dot(mixed[...], output_weight[...], preferred_element_type=jnp.float32)
    flip = (lax.axis_index("lat") >= levels).astype(jnp.int32)
    for q in range(NLAT):
        for r in range(rows):
            for s in range(cols // 8):
                at = q * places + r * cols + 8 * s
                row = r + flip * (rows - 1 - 2 * r)
                group, first = divmod(8 * s, GROUP)
                start = (row * NLAT + q) * cols + first * low + group
                for lane in range(0, width, 128):
                    shown[lane // 128, pl.ds(start, 8, stride=low), :] = (
                        folded[at : at + 8, lane : lane + 128] + lat[q : q + 1, lane : lane + 128]
                    )
    for lane in range(0, width, 128):
        v = shown[lane // 128].astype(out.dtype)
        out[:, :, :, lane : lane + 128] = v.reshape(rows, NLAT, cols, 128)


def fold(xs, gain, latents, memory_weight, output_weight):
    rows, cols, width = xs[0].shape
    places = rows * cols
    vmem = pl.BlockSpec(memory_space=pltpu.VMEM)
    params = pltpu.CompilerParams(vmem_limit_bytes=VMEM_LIMIT)
    gain, latents, memory_weight, output_weight = map(
        placed, (gain, latents, memory_weight, output_weight)
    )
    *early, late = map(placed, xs)
    before = pl.pallas_call(
        project_kernel,
        out_shape=pltpu.VMEM((len(early), places, 2 * width), jnp.bfloat16),
        in_specs=[vmem] * (len(early) + 2),
        out_specs=vmem,
        compiler_params=params,
        cost_estimate=pl.CostEstimate(
            flops=4 * len(early) * places * width * width,
            bytes_accessed=2_000_000,
            transcendentals=0,
        ),
        name="project",
    )(*early, gain, memory_weight)
    return pl.pallas_call(
        fold_kernel,
        out_shape=jax.ShapeDtypeStruct((rows, NLAT, cols, width), jnp.bfloat16),
        in_specs=[vmem] * 6,
        out_specs=vmem,
        scratch_shapes=[
            pltpu.VMEM((places, 2 * width), jnp.bfloat16),
            pltpu.VMEM((NLAT * places, width), jnp.bfloat16),
            pltpu.VMEM((width // 128, NLAT * places, 128), jnp.float32),
        ],
        compiler_params=params,
        cost_estimate=pl.CostEstimate(
            flops=8 * places * width * width, bytes_accessed=2_000_000, transcendentals=0
        ),
        name="fold",
    )(placed(before), late, gain, latents, memory_weight, output_weight)


def fits(mesh, shapes):
    pixels, embed_weight, depth, up = shapes[0], shapes[1], shapes[3], shapes[5]
    micro, levels, _, height, wide = pixels
    lat, segment = mesh.shape["lat"], mesh.shape["segment"]
    rows, cols = height // PATCH, wide // PATCH
    blocks = depth[0] // 2 * depth[1]
    return (
        segment == 4
        and depth[0] == segment
        and micro == segment
        and micro * levels == 2 * lat
        and rows == 2 * lat
        and rows == 4 * blocks
        and cols % 32 == 0
        and wide == 128
        and lat == 2 * levels
        and levels & (levels - 1) == 0
        and up[2] % 256 == 0
        and embed_weight[1] % 256 == 0
    )


def on_columns(
    pixels,
    embed_weight,
    level_code,
    depth_kernel,
    norm_gain,
    up_weight,
    up_bias,
    down_weight,
    down_bias,
    fold_gain,
    latents,
    memory_weight,
    output_weight,
):
    lat = lax.axis_size("lat")
    micro, levels, variables, height, wide = pixels.shape
    cols = wide // PATCH
    width = embed_weight.shape[1]

    swap = [(0, 1), (1, 0), (2, 3), (3, 2)]
    own = (depth_kernel[0].transpose(1, 0, 2), norm_gain[0], up_bias[0], down_bias[0])
    own = (*own, up_weight[0], down_weight[0])
    oth = tuple(lax.ppermute(w, "segment", swap) for w in own)
    got = lax.all_to_all(
        pixels.reshape(2, lat, variables, height, wide), "lat", 1, 1, tiled=True
    )

    got, oth = lax.optimization_barrier((got, oth))

    onward = [(0, 2), (1, 3)]
    across = [(2, 3), (3, 2)]
    sent = []
    for i in range(2):
        if i == 0:
            a, *weights, by_col = stage("first", (got[i],), cols, (*own, *oth, embed_weight, level_code))
        else:
            (a,) = stage("near", (got[i], by_col), cols, weights)
            a, sent[0] = lax.optimization_barrier((a, sent[0]))
        sent.append(lax.ppermute(a, "segment", onward))
    done = []
    for i in range(2):
        if i:
            done[0], sent[i] = lax.optimization_barrier((done[0], sent[i]))
        other = lax.ppermute(sent[i], "segment", across)
        (a,) = stage("far", (sent[i], other), cols, weights)
        done.append(a)
    home = lax.ppermute(done[0], "segment", [(j, i) for i, j in onward])

    pieces = []
    leaving = choose(home, done[1], levels)
    for t in reversed(range(levels)):
        pairs = []
        for s in range(4):
            for l in range(lat):
                k = (l % levels) ^ t
                to_lat = k if s % 2 == 0 else lat - 1 - k
                to_seg = 2 * (s // 2) + l // levels
                pairs.append((s * lat + l, to_seg * lat + to_lat))
        pieces.append(lax.ppermute(leaving[t], ("segment", "lat"), pairs))
    folded = fold(pieces, fold_gain[None, :], latents, memory_weight, output_weight)
    return folded.transpose(0, 2, 1, 3)[None]


def solution(mesh):
    specs = (
        P(None, None, None, "lat", None),
        P(),
        P(),
        P("segment", None, None, None),
        P("segment", None, None),
        P("segment", None, None, None),
        P("segment", None, None),
        P("segment", None, None, None),
        P("segment", None, None),
        P(),
        P(),
        P(),
        P(),
    )

    def program(*arrays):
        body = on_columns if fits(mesh, [a.shape for a in arrays]) else on_device

        return jax.shard_map(
            body,
            mesh=mesh,
            in_specs=specs,
            out_specs=P("segment", "lat", None, None, None),
            check_vma=False,
        )(*arrays)

    return program
```
